512 devices in a mesh: dom: 128 (over y, z, core), scen: 4 (over x).
Axes of the slice: x: 4, y: 8, z: 8, core: 2. Of those that a mesh axis runs over, the one named last changes fastest.
Arguments:
- embedding: bfloat16 [1310720, 256], P(('dom', 'scen')), may hold values from -6 to 6
- scenario_feats: bfloat16 [16, 1310720], P(None, ('dom', 'scen')), may hold values from -6 to 6
- adjacency: bfloat16 [10240, 2, 128, 128], P(('dom', 'scen')), may hold values from -0.3125 to 0.3125
- driver_weight: bfloat16 [1310720, 128], P(('dom', 'scen')), may hold values from -0.3125 to 0.3125
- local_slot: int32 [10240], P(('dom', 'scen')), may hold values from 0 to 79, as said below
- halo_slot: int32 [10240], P(('dom', 'scen')), may hold values from 0 to 15, as said below
- send_rows: int32 [65536, 16], P(('dom', 'scen')), may hold values from 0 to 2559
- send_count: int32 [65536], P(('dom', 'scen')), may hold values from 1 to 16, as said below
- hot_ids: int32 [128], replicated, may hold values from 0 to 1310719, as said below
- first_weight: bfloat16 [512, 256], P('scen'), may hold values from -0.25 to 0.25
- feature_weight: bfloat16 [16, 256], replicated, may hold values from -1.5 to 1.5
- first_bias: float32 [256], replicated, may hold values from -3 to 3
- second_weight: bfloat16 [256, 256], P('scen'), may hold values from -0.375 to 0.375
- second_bias: float32 [256], replicated, may hold values from -3 to 3
Outputs:
- updated: bfloat16 [1310720, 256], P(('dom', 'scen'))
The draws below stay inside these ranges and needn't reach their ends.
Inputs may be any that keep to these rules, and one draw needn't show every extreme that they name: `local_slot`: the 20 entries of one device are distinct and name exactly 5 tiles of each device of its partition; values s * 20 to s * 20 + 19 are tiles of scen index s. `halo_slot`: the entries of one device name every halo tile at least once. `send_count`: every device has a partition to which it sends 16 pins. `hot_ids`: no device holds more than 1 of them, and some device holds exactly that many.
All inputs are finite; a program needn't handle non-finite values.
Results may differ from the reference program's by a relative error of at most 0.0038.
Values may be sent and summed in bfloat16 or wider, within the bound.
No kernel may reach another device: no remote copies, remote signals or barrier semaphores. Data moves between devices by JAX's collectives and lax.ppermute only.
A program may use at most 64 MiB of HBM per device.

```python
import jax
import jax.numpy as jnp
from jax import lax

WIDTH = 256
FEAT = 16
TILE = 128
HOT = 128
HALO_TILES = 16
TILES = 20
ROWS = 2560
PINS = 1310720
CAP = 16
LOCAL_CAP = 5
N_DOM = 128
N_SCEN = 4
DEVICES = 512


def draw_local_slot(key, part):
    keys = jax.random.split(jax.random.fold_in(key, 11), DEVICES * N_SCEN)
    picks = jax.vmap(lambda k: jax.random.permutation(k, TILES)[:LOCAL_CAP])(keys)
    picks = picks.reshape(DEVICES, N_SCEN, LOCAL_CAP) + (jnp.arange(N_SCEN, dtype=jnp.int32) * TILES)[None, :, None]
    picks = picks.reshape(DEVICES, TILES)
    orders = jax.random.split(jax.random.fold_in(key, 12), DEVICES)
    mixed = jax.vmap(lambda k, r: jax.random.permutation(k, r))(orders, picks)
    return mixed.reshape(-1).astype(jnp.int32)


def draw_halo_slot(key, part):
    keys = jax.random.split(jax.random.fold_in(key, 21), DEVICES)

    def single(k):
        first, second, third = jax.random.split(k, 3)
        base = jax.random.permutation(first, HALO_TILES)
        extra = jax.random.randint(second, (TILES - HALO_TILES,), 0, HALO_TILES)
        return jax.random.permutation(third, jnp.concatenate([base, extra]))
    return jax.vmap(single)(keys).reshape(-1).astype(jnp.int32)


def draw_send_count(key, part):
    first, second = jax.random.split(jax.random.fold_in(key, 31))
    counts = jax.random.randint(first, (DEVICES, N_DOM), 1, CAP + 1)
    fullest = jax.random.randint(second, (DEVICES,), 0, N_DOM)
    counts = jnp.where(jnp.arange(N_DOM)[None, :] == fullest[:, None], CAP, counts)
    return counts.reshape(-1).astype(jnp.int32)


def draw_hot_ids(key, part):
    first, second = jax.random.split(jax.random.fold_in(key, 41))
    owners = jax.random.permutation(first, DEVICES)[jnp.arange(HOT) % DEVICES]
    within = jax.random.randint(second, (HOT,), 0, ROWS)
    return (owners * ROWS + within).astype(jnp.int32)


def place_ends(entries, own_key, low, top_value):
    dims = entries.shape
    place = [jax.random.randint(jax.random.fold_in(own_key, axis), (), 0, dims[axis]) for axis in range(len(dims))]
    entries = entries.at[tuple(place)].set(low)
    longest = dims.index(max(dims))
    place[longest] = (place[longest] + 1) % dims[longest]
    return entries.at[tuple(place)].set(top_value)


def steps_of(stream_key, extent, cuts, low, largest):
    level, own = 1.0, jax.random.fold_in(stream_key, 6)
    for axis_at, blocks in cuts:
        draws = jnp.exp(jax.random.uniform(jax.random.fold_in(own, axis_at), (blocks,), jnp.float32, low / len(cuts), largest / len(cuts)))
        level = level * jnp.repeat(draws, extent[axis_at] // blocks).reshape([-1 if axis == axis_at else 1 for axis in range(len(extent))])
    return level


def centred(stream_key, extent, width, most, cuts=(), kind=jnp.bfloat16):
    values = width * jax.random.normal(stream_key, extent, jnp.float32)
    if cuts:
        values = values * steps_of(stream_key, extent, cuts, -0.22, 0.18)
    return jnp.clip(values, -most, most).astype(kind)


def setup_inputs(seed: int = 0) -> dict:
    key_list = jax.random.split(jax.random.key(seed), 15)
    embedding = centred(key_list[0], (PINS, WIDTH), 1.0, 6.0, ((0, 512),))
    scenario_feats = centred(key_list[1], (FEAT, PINS), 1.0, 6.0, ((1, 512),))
    adjacency = centred(key_list[2], (PINS // TILE, 2, TILE, TILE), (3 * TILE) ** -0.5, 0.3125, ((0, 512),))
    driver_weight = centred(key_list[3], (PINS, HOT), (3 * TILE) ** -0.5, 0.3125, ((0, 512),))
    local_slot = draw_local_slot(jax.random.fold_in(key_list[14], 71), 0)
    halo_slot = draw_halo_slot(jax.random.fold_in(key_list[14], 71), 0)
    send_rows = place_ends(jax.random.randint(key_list[6], (DEVICES * N_DOM, CAP), 0, ROWS), jax.random.fold_in(key_list[6], 1), 0, ROWS - 1).astype(jnp.int32)
    send_count = draw_send_count(jax.random.fold_in(key_list[14], 71), 0)
    hot_ids = draw_hot_ids(jax.random.fold_in(key_list[14], 71), 0)
    first_weight = centred(key_list[9], (2 * WIDTH, WIDTH), (2 * WIDTH) ** -0.5, 0.25, ((0, 4),))
    feature_weight = centred(key_list[10], (FEAT, WIDTH), FEAT ** -0.5, 1.5)
    first_bias = centred(key_list[11], (WIDTH,), 0.5, 3.0, (), jnp.float32)
    second_weight = centred(key_list[12], (WIDTH, WIDTH), WIDTH ** -0.5, 0.375, ((0, 4),))
    second_bias = centred(key_list[13], (WIDTH,), 0.5, 3.0, (), jnp.float32)
    return dict(embedding=embedding, scenario_feats=scenario_feats, adjacency=adjacency, driver_weight=driver_weight, local_slot=local_slot, halo_slot=halo_slot, send_rows=send_rows, send_count=send_count, hot_ids=hot_ids, first_weight=first_weight, feature_weight=feature_weight, first_bias=first_bias, second_weight=second_weight, second_bias=second_bias)


def reference(embedding, scenario_feats, adjacency, driver_weight, local_slot, halo_slot, send_rows, send_count, hot_ids, first_weight, feature_weight, first_bias, second_weight, second_bias):
    rows = TILES * TILE
    drivers = embedding[hot_ids]
    send_view = send_rows.reshape(DEVICES, N_DOM, CAP)
    count_view = send_count.reshape(DEVICES, N_DOM)

    def device(index):
        domain = index // N_SCEN
        group = index - domain * N_SCEN
        own = lax.dynamic_slice_in_dim(embedding, index * rows, rows, 0)
        partition = lax.dynamic_slice_in_dim(embedding, domain * N_SCEN * rows, N_SCEN * rows, 0).reshape(N_SCEN * TILES, TILE, WIDTH)
        slots = lax.dynamic_slice_in_dim(local_slot, index * TILES, TILES, 0)
        local_tiles = partition[slots].astype(jnp.float32)
        peers = jnp.arange(N_DOM, dtype=jnp.int32) * N_SCEN + group
        chosen = send_view[peers, domain]
        counts = count_view[peers, domain]
        live = jnp.arange(CAP, dtype=jnp.int32)[None, :] < counts[:, None]
        flat = (peers[:, None] * rows + chosen).astype(jnp.int32)
        halo = jnp.where(live[:, :, None], embedding[flat].astype(jnp.float32), jnp.float32(0.0))
        halo = halo.reshape(HALO_TILES, TILE, WIDTH)
        halo_tiles = halo[lax.dynamic_slice_in_dim(halo_slot, index * TILES, TILES, 0)]
        blocks = lax.dynamic_slice_in_dim(adjacency, index * TILES, TILES, 0).astype(jnp.float32)
        summed = jnp.einsum("tij,tjc->tic", blocks[:, 0], local_tiles)
        summed = summed + jnp.einsum("tij,tjc->tic", blocks[:, 1], halo_tiles)
        weights_hot = lax.dynamic_slice_in_dim(driver_weight, index * rows, rows, 0)
        summed = summed.reshape(rows, WIDTH) + jnp.dot(weights_hot, drivers, preferred_element_type=jnp.float32)
        aggregate = summed.astype(jnp.bfloat16)
        joined = jnp.concatenate([own, aggregate], axis=1)
        feats = lax.dynamic_slice_in_dim(scenario_feats, index * rows, rows, 1)
        inner = jnp.dot(joined, first_weight, preferred_element_type=jnp.float32)
        inner = inner + jnp.dot(feats.T, feature_weight, preferred_element_type=jnp.float32) + first_bias
        activated = jax.nn.gelu(inner, approximate=False).astype(jnp.bfloat16)
        result = own.astype(jnp.float32) + jnp.dot(activated, second_weight, preferred_element_type=jnp.float32) + second_bias
        return result.astype(jnp.bfloat16)

    outputs = lax.map(device, jnp.arange(DEVICES, dtype=jnp.int32))
    return outputs.reshape(DEVICES * rows, WIDTH)
```

```python
import jax
import jax.numpy as jnp
from jax import lax
from jax.experimental import pallas as pl
from jax.experimental.pallas import tpu as pltpu
from jax.sharding import PartitionSpec as P

BF16, F32, I32 = jnp.bfloat16, jnp.float32, jnp.int32
VMEM_BYTES = 48 * 1024 * 1024
NOTE = 16


def _params(**more):
    return pltpu.CompilerParams(vmem_limit_bytes=VMEM_BYTES, **more)


def _dot(a, b):
    return jnp.dot(a, b, preferred_element_type=F32)


def note(myself, hot_ids, local_slot, embedding, groups):
    rows, width = embedding.shape
    hots, tiles = hot_ids.shape[0], local_slot.shape[0]

    def body(myself_ref, hot_ref, slot_ref, emb_ref, out_ref, block, page, sem):
        within = hot_ref[...] - myself_ref[0] * rows
        row = jnp.max(jnp.where((within >= 0) & (within < rows), within, -1))
        start = pl.multiple_of((jnp.maximum(row, 0) // NOTE) * NOTE, NOTE)
        copy = pltpu.make_async_copy(emb_ref.at[pl.ds(start, NOTE), :], block, sem)
        copy.start()
        page[...] = jnp.zeros((NOTE, width), F32)
        page[1:2, :tiles] = slot_ref[...].astype(F32)
        copy.wait()
        at = lax.broadcasted_iota(I32, (NOTE, width), 0)
        mine = jnp.where(at == row - start, block[...].astype(F32), 0.0)
        page[0:1, :] = jnp.sum(mine, axis=0, keepdims=True)
        out_ref[...] = jnp.broadcast_to(page[...].astype(BF16)[None], (groups, NOTE, width))

    return pl.pallas_call(
        body,
        out_shape=jax.ShapeDtypeStruct((groups, NOTE, width), BF16),
        in_specs=[
            pl.BlockSpec(memory_space=pltpu.SMEM),
            pl.BlockSpec((1, hots), lambda: (0, 0)),
            pl.BlockSpec((1, tiles), lambda: (0, 0)),
            pl.BlockSpec(memory_space=pl.ANY),
        ],
        out_specs=pl.BlockSpec((groups, NOTE, width), lambda: (0, 0, 0)),
        scratch_shapes=[
            pltpu.VMEM((NOTE, width), BF16),
            pltpu.VMEM((NOTE, width), F32),
            pltpu.SemaphoreType.DMA(()),
        ],
        compiler_params=_params(),
        name="note",
    )(myself, hot_ids.reshape(1, hots), local_slot.reshape(1, tiles), embedding)


def pick_rows(send_rows, send_count, embedding):
    rows, width = embedding.shape
    doms, cap = send_rows.shape
    half = width // 2
    step = 32
    parts = rows // 128

    def body(rows_ref, count_ref, emb_ref, out_ref, chosen):
        slot = lax.broadcasted_iota(I32, (cap, doms), 0)
        index = jnp.where(slot < count_ref[...], rows_ref[...], -1)
        lane = lax.broadcasted_iota(I32, (cap, 128), 1).astype(F32).astype(BF16)
        one, zero = jnp.ones((), BF16), jnp.zeros((), BF16)

        def some(i, _):
            turned = pltpu.roll(index, (doms - i * step) % doms, 1)
            low = (turned & 127).astype(F32)
            high = (turned >> 7).astype(F32)
            for p in range(step):
                low_p = jnp.broadcast_to(low[:, p : p + 1], (cap, 128)).astype(BF16)
                high_p = jnp.broadcast_to(high[:, p : p + 1], (cap, 128)).astype(BF16)
                at = jnp.where(low_p == lane, one, zero)
                for k in range(parts):
                    chosen[p * cap : (p + 1) * cap, k * 128 : (k + 1) * 128] = jnp.where(
                        high_p == jnp.asarray(k, BF16), at, zero
                    )
            got = _dot(chosen[...], emb_ref[...]).astype(BF16).reshape(step, cap, width)
            here = pl.ds(pl.multiple_of(i * step, step), step)
            out_ref[here, :cap, :] = got[:, :, :half]
            out_ref[here, cap : 2 * cap, :] = got[:, :, half:]
            out_ref[here, 2 * cap :, :] = jnp.zeros((step, 8, half), BF16)
            return 0

        lax.fori_loop(0, doms // step, some, 0)

    return pl.pallas_call(
        body,
        out_shape=jax.ShapeDtypeStruct((doms, 2 * cap + 8, half), BF16),
        in_specs=[
            pl.BlockSpec((cap, doms), lambda: (0, 0)),
            pl.BlockSpec((1, doms), lambda: (0, 0)),
            pl.BlockSpec((rows, width), lambda: (0, 0)),
        ],
        out_specs=pl.BlockSpec((doms, 2 * cap + 8, half), lambda: (0, 0, 0)),
        scratch_shapes=[pltpu.VMEM((step * cap, rows), BF16)],
        compiler_params=_params(),
        name="pick_rows",
    )(send_rows.T, send_count.reshape(1, doms), embedding)


def add_drivers(notes, message):
    doms, length, half = message.shape
    groups = notes.shape[0]

    def body(notes_ref, _, out_ref, page, sem):
        at = lax.broadcasted_iota(I32, (8, half), 0)
        last = jnp.zeros((8, half), F32)
        for g in range(groups):
            row = notes_ref[g].astype(F32)[0:1, :]
            last = jnp.where(at == g, row[:, :half], last)
            last = jnp.where(at == groups + g, row[:, half:], last)
        page[...] = jnp.broadcast_to(last[None], (doms, 8, half)).astype(BF16)
        copy = pltpu.make_async_copy(page, out_ref.at[:, pl.ds(length - 8, 8), :], sem)
        copy.start()
        copy.wait()

    return pl.pallas_call(
        body,
        out_shape=jax.ShapeDtypeStruct(message.shape, BF16),
        in_specs=[pl.BlockSpec(notes.shape, lambda: (0, 0, 0)), pl.BlockSpec(memory_space=pl.ANY)],
        out_specs=pl.BlockSpec(memory_space=pl.ANY),
        scratch_shapes=[pltpu.VMEM((doms, 8, half), BF16), pltpu.SemaphoreType.DMA(())],
        input_output_aliases={1: 0},
        compiler_params=_params(),
        name="add_drivers",
    )(notes, message)


def pick_tiles(group, slots, embedding, first_weight, second_weight, tile):
    groups, tiles = slots.shape
    rows, width = embedding.shape
    each = tiles // groups
    a, b = first_weight.shape[0], second_weight.shape[0]
    length = each * tile + a + b

    def body(group_ref, slots_ref, emb_ref, first_ref, second_ref, *rest):
        outs, (listed, sems) = rest[: groups - 1], rest[groups - 1 :]
        me = group_ref[0]
        copies = []
        for k in range(1, groups):
            out = outs[k - 1]
            other = (me + k) % groups
            copies.append(pltpu.make_async_copy(first_ref, out.at[pl.ds(each * tile, a), :], sems.at[k - 1, each]))
            copies.append(
                pltpu.make_async_copy(second_ref, out.at[pl.ds(each * tile + a, b), :], sems.at[k - 1, each + 1])
            )
            for j in range(each):
                listed[k - 1, j] = 0

            def look(t, found, k=k, other=other):
                tile_at = slots_ref[other, t]
                hit = tile_at // tiles == me

                @pl.when(hit)
                def _():
                    listed[k - 1, jnp.minimum(found, each - 1)] = tile_at - me * tiles

                return found + hit.astype(I32)

            lax.fori_loop(0, tiles, look, jnp.zeros((), I32))
            for j in range(each):
                start = pl.multiple_of(listed[k - 1, j] * tile, tile)
                copies.append(
                    pltpu.make_async_copy(
                        emb_ref.at[pl.ds(start, tile), :], out.at[pl.ds(j * tile, tile), :], sems.at[k - 1, j]
                    )
                )
        for copy in copies:
            copy.start()
        for copy in copies:
            copy.wait()

    hbm = pl.BlockSpec(memory_space=pl.ANY)
    smem = pl.BlockSpec(memory_space=pltpu.SMEM)
    return pl.pallas_call(
        body,
        out_shape=[jax.ShapeDtypeStruct((length, width), BF16)] * (groups - 1),
        in_specs=[smem, smem, hbm, hbm, hbm],
        out_specs=[hbm] * (groups - 1),
        scratch_shapes=[
            pltpu.SMEM((groups - 1, each), I32),
            pltpu.SemaphoreType.DMA((groups - 1, each + 2)),
        ],
        compiler_params=_params(),
        name="pick_tiles",
    )(group, slots, embedding, first_weight, second_weight)


def before_halo(
    group, slot, embedding, arrived, first_weight, second_weight, adjacency, feats, feature_weight, first_bias
):
    rows, width = embedding.shape
    tiles, _, tile, _ = adjacency.shape
    groups = len(arrived) + 1
    each = tiles // groups
    a, b = first_weight.shape[0], second_weight.shape[0]
    many = 2
    block = many * tile

    def body(group_ref, slot_ref, emb_ref, own_a, own_b, adj_ref, feat_ref, fw_ref, bias_ref, *rest):
        parts = rest[: groups - 1]
        local_ref, start_ref, lower_ref, second_ref, weight, got, place = rest[groups - 1 :]
        me = group_ref[0]
        i = pl.program_id(0)

        @pl.when(i == 0)
        def _():
            mine_a, mine_b = pl.ds(pl.multiple_of(me * a, a), a), pl.ds(pl.multiple_of(me * b, b), b)
            weight[mine_a, :] = own_a[...]
            second_ref[mine_b, :] = own_b[...]
            for k in range(1, groups):
                other = (me + groups - k) % groups
                there_a = pl.ds(pl.multiple_of(other * a, a), a)
                there_b = pl.ds(pl.multiple_of(other * b, b), b)
                weight[there_a, :] = parts[k - 1][each * tile : each * tile + a, :]
                second_ref[there_b, :] = parts[k - 1][each * tile + a :, :]
            lower_ref[...] = weight[width:, :]

            def number(t, counts):
                source = slot_ref[t] // tiles
                spot = sum(jnp.where(source == g, counts[g], 0) for g in range(groups))
                place[t] = spot
                return tuple(counts[g] + (source == g).astype(I32) for g in range(groups))

            lax.fori_loop(0, tiles, number, (jnp.zeros((), I32),) * groups)

        for u in range(many):
            t = i * many + u
            source = slot_ref[t] // tiles
            away = (me + groups - source) % groups

            @pl.when(away == 0)
            def _():
                at = pl.multiple_of((slot_ref[t] - source * tiles) * tile, tile)
                got[...] = emb_ref[pl.ds(at, tile), :]

            for k in range(1, groups):

                @pl.when(away == k)
                def _(k=k):
                    at = pl.multiple_of(jnp.minimum(place[t], each - 1) * tile, tile)
                    got[...] = parts[k - 1][pl.ds(at, tile), :]

            local_ref[u * tile : (u + 1) * tile, :] = _dot(adj_ref[u, 0], got[...])
        own = emb_ref[pl.ds(pl.multiple_of(i * block, block), block), :]
        start_ref[...] = (
            _dot(own, weight[:width, :])
            + lax.dot_general(feat_ref[...], fw_ref[...], (((0,), (0,)), ((), ())), preferred_element_type=F32)
            + bias_ref[...]
        )

    def whole(x):
        return pl.BlockSpec(x.shape, lambda i, *_: (0,) * x.ndim)

    f32_rows = jax.ShapeDtypeStruct((rows, width), F32)
    square = jax.ShapeDtypeStruct((width, width), BF16)
    by_rows = pl.BlockSpec((block, width), lambda i, *_: (i, 0))
    fixed = pl.BlockSpec((width, width), lambda i, *_: (0, 0))
    return pl.pallas_call(
        body,
        out_shape=[f32_rows, f32_rows, square, square],
        grid_spec=pltpu.PrefetchScalarGridSpec(
            num_scalar_prefetch=2,
            grid=(tiles // many,),
            in_specs=[
                whole(embedding),
                whole(first_weight),
                whole(second_weight),
                pl.BlockSpec((many, 1, tile, tile), lambda i, *_: (i, 0, 0, 0)),
                pl.BlockSpec((feats.shape[0], block), lambda i, *_: (0, i)),
                whole(feature_weight),
                whole(first_bias),
                *[whole(x) for x in arrived],
            ],
            out_specs=[by_rows, by_rows, fixed, fixed],
            scratch_shapes=[
                pltpu.VMEM((2 * width, width), BF16),
                pltpu.VMEM((tile, width), BF16),
                pltpu.SMEM((tiles,), I32),
            ],
        ),
        compiler_params=_params(),
        name="before_halo",
    )(group, slot, embedding, first_weight, second_weight, adjacency, feats, feature_weight, first_bias, *arrived)


def after_halo(
    halo_slot, halo, driver_at, local, start, adjacency, driver_weight, embedding, lower, second, second_bias
):
    rows, width = embedding.shape
    tiles, _, tile, _ = adjacency.shape
    doms, length, half = halo.shape
    cap = (length - 8) // 2
    hots = driver_weight.shape[1]
    many = 2
    block = many * tile
    per = tile // cap

    def body(
        slot_ref, halo_ref, at_ref, local_ref, start_ref, adj_ref, dw_ref, emb_ref, lower_ref, second_ref, bias_ref,
        out_ref, drivers, summed,
    ):
        i = pl.program_id(0)

        @pl.when(i == 0)
        def _():
            column = lax.broadcasted_iota(I32, (hots, doms * 8), 1)
            ends = halo_ref[:, 2 * cap :, :].reshape(doms * 8, half)
            left = jnp.where(column == at_ref[...], 1.0, 0.0).astype(BF16)
            right = jnp.where(column == at_ref[...] + 4, 1.0, 0.0).astype(BF16)
            drivers[:, :half] = _dot(left, ends).astype(BF16)
            drivers[:, half:] = _dot(right, ends).astype(BF16)

        for u in range(many):
            which = pl.ds(pl.multiple_of(slot_ref[i * many + u] * per, per), per)
            here = slice(u * tile, (u + 1) * tile)
            summed[here, :half] = local_ref[here, :half] + _dot(
                adj_ref[u, 0], halo_ref[which, :cap, :].reshape(tile, half)
            )
            summed[here, half:] = local_ref[here, half:] + _dot(
                adj_ref[u, 0], halo_ref[which, cap : 2 * cap, :].reshape(tile, half)
            )
        aggregate = (summed[...] + _dot(dw_ref[...], drivers[...])).astype(BF16)
        inner = start_ref[...] + _dot(aggregate, lower_ref[...])
        activated = (0.5 * inner * (1.0 + lax.erf(inner * (0.5**0.5)))).astype(BF16)
        out_ref[...] = (emb_ref[...].astype(F32) + bias_ref[...] + _dot(activated, second_ref[...])).astype(BF16)

    def whole(x):
        return pl.BlockSpec(x.shape, lambda i, *_: (0,) * x.ndim)

    by_rows = pl.BlockSpec((block, width), lambda i, *_: (i, 0))
    return pl.pallas_call(
        body,
        out_shape=jax.ShapeDtypeStruct((rows, width), BF16),
        grid_spec=pltpu.PrefetchScalarGridSpec(
            num_scalar_prefetch=1,
            grid=(tiles // many,),
            in_specs=[
                whole(halo),
                whole(driver_at),
                by_rows,
                by_rows,
                pl.BlockSpec((many, 1, tile, tile), lambda i, *_: (i, 1, 0, 0)),
                pl.BlockSpec((block, hots), lambda i, *_: (i, 0)),
                by_rows,
                whole(lower),
                whole(second),
                whole(second_bias),
            ],
            out_specs=by_rows,
            scratch_shapes=[pltpu.VMEM((hots, width), BF16), pltpu.VMEM((block, width), F32)],
        ),
        compiler_params=_params(),
        name="after_halo",
    )(halo_slot, halo, driver_at, local, start, adjacency, driver_weight, embedding, lower, second, second_bias)


def per_device(
    embedding,
    scenario_feats,
    adjacency,
    driver_weight,
    local_slot,
    halo_slot,
    send_rows,
    send_count,
    hot_ids,
    first_weight,
    feature_weight,
    first_bias,
    second_weight,
    second_bias,
):
    rows, width = embedding.shape
    tile = adjacency.shape[-1]
    tiles = rows // tile
    groups = lax.axis_size("scen")
    myself = lax.axis_index(("dom", "scen")).astype(I32).reshape(1)
    group = lax.axis_index("scen").astype(I32).reshape(1)

    page = note(myself, hot_ids, local_slot, embedding, groups)
    notes = lax.all_to_all(page, "scen", split_axis=0, concat_axis=0, tiled=True)
    message = pick_rows(send_rows, send_count, embedding)
    message = add_drivers(notes, message)
    halo = lax.all_to_all(message, "dom", split_axis=0, concat_axis=0, tiled=True)

    slots = notes[:, 1, :tiles].astype(I32)
    leaving = pick_tiles(group, slots, embedding, first_weight, second_weight, tile)
    arrived = [
        lax.ppermute(x, "scen", [(g, (g + k) % groups) for g in range(groups)])
        for k, x in enumerate(leaving, start=1)
    ]
    local, start, lower, second = before_halo(
        group,
        local_slot,
        embedding,
        arrived,
        first_weight,
        second_weight,
        adjacency,
        scenario_feats,
        feature_weight,
        first_bias.reshape(1, width),
    )
    owner = hot_ids // rows
    driver_at = (owner // groups * 8 + owner % groups).reshape(-1, 1)
    return after_halo(
        halo_slot,
        halo,
        driver_at,
        local,
        start,
        adjacency,
        driver_weight,
        embedding,
        lower,
        second,
        second_bias.reshape(1, width),
    )


def solution(mesh):
    return jax.shard_map(
        per_device,
        mesh=mesh,
        in_specs=(
            P(("dom", "scen"), None),
            P(None, ("dom", "scen")),
            P(("dom", "scen"), None, None, None),
            P(("dom", "scen"), None),
            P(("dom", "scen")),
            P(("dom", "scen")),
            P(("dom", "scen"), None),
            P(("dom", "scen")),
            P(),
            P("scen", None),
            P(),
            P(),
            P("scen", None),
            P(),
        ),
        out_specs=P(("dom", "scen"), None),
        check_vma=False,
    )
```

```python
import jax
import jax.numpy as jnp
from jax import lax
from jax.experimental import pallas as pl
from jax.experimental.pallas import tpu as pltpu
from jax.sharding import PartitionSpec as P

BF16, F32, I32 = jnp.bfloat16, jnp.float32, jnp.int32
NOTE = 16


def _params(mebibytes):
    return pltpu.CompilerParams(vmem_limit_bytes=mebibytes * 1024 * 1024)


def _near(x):
    return pltpu.with_memory_space_constraint(x, pltpu.VMEM)


def _far(x):
    return pltpu.with_memory_space_constraint(x, pltpu.HBM)


def _dot(a, b):
    return jnp.dot(a, b, preferred_element_type=F32)


def note(myself, hot_ids, local_slot, embedding, groups):
    rows, width = embedding.shape
    hots, tiles = hot_ids.shape[0], local_slot.shape[0]

    def body(myself_ref, hot_hbm, slot_hbm, emb_ref, out_ref, hot_ref, slot_ref, block, page, sems):
        hot_copy = pltpu.make_async_copy(hot_hbm, hot_ref, sems.at[0])
        slot_copy = pltpu.make_async_copy(slot_hbm, slot_ref, sems.at[1])
        hot_copy.start()
        slot_copy.start()
        page[...] = jnp.zeros((NOTE, width), F32)
        hot_copy.wait()
        within = hot_ref[...] - myself_ref[0] * rows
        row = jnp.max(jnp.where((within >= 0) & (within < rows), within, -1))
        start = pl.multiple_of((jnp.maximum(row, 0) // NOTE) * NOTE, NOTE)
        copy = pltpu.make_async_copy(emb_ref.at[pl.ds(start, NOTE), :], block, sems.at[2])
        copy.start()
        slot_copy.wait()
        page[1:2, :tiles] = slot_ref[...].astype(F32)
        copy.wait()
        at = lax.broadcasted_iota(I32, (NOTE, width), 0)
        mine = jnp.where(at == row - start, block[...].astype(F32), 0.0)
        page[0:1, :] = jnp.sum(mine, axis=0, keepdims=True)
        out_ref[...] = jnp.broadcast_to(page[...].astype(BF16)[None], (groups, NOTE, width))

    hbm = pl.BlockSpec(memory_space=pltpu.HBM)
    return pl.pallas_call(
        body,
        out_shape=jax.ShapeDtypeStruct((groups, NOTE, width), BF16),
        in_specs=[pl.BlockSpec(memory_space=pltpu.SMEM), hbm, hbm, hbm],
        out_specs=pl.BlockSpec((groups, NOTE, width), lambda: (0, 0, 0)),
        scratch_shapes=[
            pltpu.VMEM((1, hots), I32),
            pltpu.VMEM((1, tiles), I32),
            pltpu.VMEM((NOTE, width), BF16),
            pltpu.VMEM((NOTE, width), F32),
            pltpu.SemaphoreType.DMA((3,)),
        ],
        compiler_params=_params(1),
        name="note",
    )(myself, _far(hot_ids.reshape(1, hots)), _far(local_slot.reshape(1, tiles)), _far(embedding))


def pick_rows(send_rows, send_count, embedding):
    rows, width = embedding.shape
    doms, cap = send_rows.shape
    half = width // 2
    step = 32
    parts = rows // 128

    def body(rows_ref, count_ref, emb_ref, out_hbm, out_ref, sems):
        slot = lax.broadcasted_iota(I32, (cap, doms), 0)
        index = jnp.where(slot < count_ref[...], rows_ref[...], -1)
        low = (index & 127).astype(F32)
        high = (index >> 7).astype(F32)
        lane = lax.broadcasted_iota(I32, (cap, 128), 1).astype(F32).astype(BF16)
        one, zero = jnp.ones((), BF16), jnp.zeros((), BF16)
        copies = []
        for i in range(0, doms, step):
            chosen = []
            for p in range(i, i + step):
                low_p = jnp.broadcast_to(low[:, p : p + 1], (cap, 128)).astype(BF16)
                high_p = jnp.broadcast_to(high[:, p : p + 1], (cap, 128)).astype(BF16)
                at = jnp.where(low_p == lane, one, zero)
                chosen.append(
                    jnp.concatenate([jnp.where(high_p == jnp.asarray(k, BF16), at, zero) for k in range(parts)], axis=1)
                )
            got = _dot(jnp.concatenate(chosen, axis=0), emb_ref[...]).astype(BF16).reshape(step, cap, width)
            out_ref[i : i + step, :cap, :] = got[:, :, :half]
            out_ref[i : i + step, cap : 2 * cap, :] = got[:, :, half:]
            copies.append(
                pltpu.make_async_copy(
                    out_ref.at[i : i + step], out_hbm.at[i : i + step, : 2 * cap, :], sems.at[i // step]
                )
            )
            copies[-1].start()
        for copy in copies:
            copy.wait()

    return pl.pallas_call(
        body,
        out_shape=pltpu.HBM((doms, 2 * cap + 8, half), BF16),
        in_specs=[
            pl.BlockSpec((cap, doms), lambda: (0, 0)),
            pl.BlockSpec((1, doms), lambda: (0, 0)),
            pl.BlockSpec((rows, width), lambda: (0, 0)),
        ],
        out_specs=pl.BlockSpec(memory_space=pl.ANY),
        scratch_shapes=[pltpu.VMEM((doms, 2 * cap, half), BF16), pltpu.SemaphoreType.DMA((doms // step,))],
        compiler_params=_params(24),
        name="pick_rows",
    )(_near(send_rows.T), _near(send_count.reshape(1, doms)), _near(embedding))


def add_drivers(notes, message):
    doms, length, half = message.shape
    groups = notes.shape[0]

    def body(notes_ref, _, out_ref, page, sem):
        at = lax.broadcasted_iota(I32, (8, half), 0)
        last = jnp.zeros((8, half), F32)
        for g in range(groups):
            row = notes_ref[g].astype(F32)[0:1, :]
            last = jnp.where(at == g, row[:, :half], last)
            last = jnp.where(at == groups + g, row[:, half:], last)
        page[...] = jnp.broadcast_to(last[None], (doms, 8, half)).astype(BF16)
        copy = pltpu.make_async_copy(page, out_ref.at[:, pl.ds(length - 8, 8), :], sem)
        copy.start()
        copy.wait()

    return pl.pallas_call(
        body,
        out_shape=jax.ShapeDtypeStruct(message.shape, BF16),
        in_specs=[pl.BlockSpec(notes.shape, lambda: (0, 0, 0)), pl.BlockSpec(memory_space=pl.ANY)],
        out_specs=pl.BlockSpec(memory_space=pl.ANY),
        scratch_shapes=[pltpu.VMEM((doms, 8, half), BF16), pltpu.SemaphoreType.DMA(())],
        input_output_aliases={1: 0},
        compiler_params=_params(2),
        name="add_drivers",
    )(notes, _far(message))


def pick_tiles(group, slots, embedding, first_weight, second_weight, tile):
    groups, tiles = slots.shape
    rows, width = embedding.shape
    each = tiles // groups
    a, b = first_weight.shape[0], second_weight.shape[0]
    length = each * tile + a + b

    def body(group_ref, slots_ref, emb_ref, first_ref, second_ref, *rest):
        outs, (listed, sems) = rest[: groups - 1], rest[groups - 1 :]
        me = group_ref[0]
        copies = []
        for k in range(1, groups):
            out = outs[k - 1]
            other = (me + k) % groups
            copies.append(pltpu.make_async_copy(first_ref, out.at[pl.ds(each * tile, a), :], sems.at[k - 1, each]))
            copies.append(
                pltpu.make_async_copy(second_ref, out.at[pl.ds(each * tile + a, b), :], sems.at[k - 1, each + 1])
            )
            for j in range(each):
                listed[k - 1, j] = 0

            def look(t, found, k=k, other=other):
                tile_at = slots_ref[other, t]
                hit = tile_at // tiles == me

                @pl.when(hit)
                def _():
                    listed[k - 1, jnp.minimum(found, each - 1)] = tile_at - me * tiles

                return found + hit.astype(I32)

            lax.fori_loop(0, tiles, look, jnp.zeros((), I32))
            for j in range(each):
                start = pl.multiple_of(listed[k - 1, j] * tile, tile)
                copies.append(
                    pltpu.make_async_copy(
                        emb_ref.at[pl.ds(start, tile), :], out.at[pl.ds(j * tile, tile), :], sems.at[k - 1, j]
                    )
                )
        for copy in copies:
            copy.start()
        for copy in copies:
            copy.wait()

    hbm = pl.BlockSpec(memory_space=pl.ANY)
    smem = pl.BlockSpec(memory_space=pltpu.SMEM)
    return pl.pallas_call(
        body,
        out_shape=[pltpu.HBM((length, width), BF16)] * (groups - 1),
        in_specs=[smem, smem, hbm, hbm, hbm],
        out_specs=[hbm] * (groups - 1),
        scratch_shapes=[
            pltpu.SMEM((groups - 1, each), I32),
            pltpu.SemaphoreType.DMA((groups - 1, each + 2)),
        ],
        compiler_params=_params(2),
        name="pick_tiles",
    )(group, slots, _near(embedding), first_weight, second_weight)


def ready(
    group, slot, embedding, arrived, first_weight, second_weight, feats, feature_weight, first_bias, tile
):
    rows, width = embedding.shape
    tiles = slot.shape[0]
    groups = len(arrived) + 1
    each = tiles // groups
    a, b = first_weight.shape[0], second_weight.shape[0]
    many = rows // 4

    def body(group_ref, slot_ref, emb_ref, own_a, own_b, feat_hbm, fw_hbm, bias_hbm, *rest):
        parts = rest[: groups - 1]
        tiles_ref, start_hbm, lower_ref, second_ref, *rest = rest[groups - 1 :]
        start_ref, weight, feat_ref, fw_ref, bias_ref, tile_sems, start_sems, sems, small_sems = rest
        me = group_ref[0]
        small = [
            pltpu.make_async_copy(feat_hbm, feat_ref, small_sems.at[0]),
            pltpu.make_async_copy(fw_hbm, fw_ref, small_sems.at[1]),
            pltpu.make_async_copy(bias_hbm, bias_ref, small_sems.at[2]),
        ]
        firsts, seconds = [], []
        for k in range(groups):
            other = (me + groups - k) % groups
            from_a = own_a if k == 0 else parts[k - 1].at[pl.ds(each * tile, a), :]
            from_b = own_b if k == 0 else parts[k - 1].at[pl.ds(each * tile + a, b), :]
            to_a = weight.at[pl.ds(pl.multiple_of(other * a, a), a), :]
            to_b = second_ref.at[pl.ds(pl.multiple_of(other * b, b), b), :]
            firsts.append(pltpu.make_async_copy(from_a, to_a, sems.at[0, k]))
            seconds.append(pltpu.make_async_copy(from_b, to_b, sems.at[1, k]))
        for copy in (*firsts, *small, *seconds):
            copy.start()

        def send(t, counts):
            source = slot_ref[t] // tiles
            spot = sum(jnp.where(source == g, counts[g], 0) for g in range(groups))
            away = (me + groups - source) % groups
            for k in range(groups):

                @pl.when(away == k)
                def _(k=k):
                    if k == 0:
                        at = pl.multiple_of((slot_ref[t] - source * tiles) * tile, tile)
                        copy = pltpu.make_async_copy(emb_ref.at[pl.ds(at, tile), :], tiles_ref.at[t], tile_sems.at[t])
                    else:
                        at = pl.multiple_of(jnp.minimum(spot, each - 1) * tile, tile)
                        here = parts[k - 1].at[pl.ds(at, tile), :]
                        copy = pltpu.make_async_copy(here, tiles_ref.at[t], tile_sems.at[t])
                    copy.start()

            return tuple(counts[g] + (source == g).astype(I32) for g in range(groups))

        lax.fori_loop(0, tiles, send, (jnp.zeros((), I32),) * groups)
        for copy in (*firsts, *small):
            copy.wait()
        leaving = [pltpu.make_async_copy(weight.at[pl.ds(width, width), :], lower_ref, small_sems.at[0])]
        leaving[0].start()
        for n in range(rows // many):
            here = pl.ds(n * many, many)
            start_ref[here, :] = (
                _dot(emb_ref[here, :], weight[:width, :])
                + lax.dot_general(
                    feat_ref[:, n * many : (n + 1) * many],
                    fw_ref[...],
                    (((0,), (0,)), ((), ())),
                    preferred_element_type=F32,
                )
                + bias_ref[...]
            )
            leaving.append(pltpu.make_async_copy(start_ref.at[here, :], start_hbm.at[here, :], start_sems.at[n]))
            leaving[-1].start()
        for copy in (*seconds, *leaving):
            copy.wait()
        for t in range(tiles):
            pltpu.make_async_copy(emb_ref.at[pl.ds(0, tile), :], tiles_ref.at[t], tile_sems.at[t]).wait()

    smem = pl.BlockSpec(memory_space=pltpu.SMEM)
    hbm = pl.BlockSpec(memory_space=pltpu.HBM)
    return pl.pallas_call(
        body,
        out_shape=[
            pltpu.HBM((tiles, tile, width), BF16),
            pltpu.HBM((rows, width), F32),
            pltpu.HBM((width, width), BF16),
            pltpu.HBM((width, width), BF16),
        ],
        in_specs=[smem, smem, pl.BlockSpec(memory_space=pltpu.VMEM)] + [hbm] * (5 + len(arrived)),
        out_specs=[hbm] * 4,
        scratch_shapes=[
            pltpu.VMEM((rows, width), F32),
            pltpu.VMEM((2 * width, width), BF16),
            pltpu.VMEM(feats.shape, BF16),
            pltpu.VMEM(feature_weight.shape, BF16),
            pltpu.VMEM(first_bias.shape, F32),
            pltpu.SemaphoreType.DMA((tiles,)),
            pltpu.SemaphoreType.DMA((rows // many,)),
            pltpu.SemaphoreType.DMA((2, groups)),
            pltpu.SemaphoreType.DMA((3,)),
        ],
        compiler_params=_params(12),
        name="ready",
    )(
        group,
        slot,
        _near(embedding),
        *map(_far, (first_weight, second_weight, feats, feature_weight, first_bias, *arrived)),
    )


def after_halo(
    halo_slot, halo, driver_at, local_tiles, start, adjacency, driver_weight, embedding, lower, second, second_bias
):
    rows, width = embedding.shape
    tiles, _, tile, _ = adjacency.shape
    doms, length, half = halo.shape
    cap = (length - 8) // 2
    hots = driver_weight.shape[1]
    many = tiles // 4
    block = many * tile
    per = tile // cap

    def body(
        halo_hbm, local_hbm, start_hbm, lower_hbm, second_hbm, slot_hbm, bias_hbm, at_ref, adj_ref, dw_ref, emb_ref,
        out_hbm, halo_ref, local_ref, start_ref, lower_ref, second_ref, slot_ref, bias_ref, out, sems, in_sems, out_sems,
    ):
        halo_copy = pltpu.make_async_copy(halo_hbm, halo_ref, sems.at[0])
        slot_copy = pltpu.make_async_copy(slot_hbm, slot_ref, sems.at[1])
        rest = [
            pltpu.make_async_copy(lower_hbm, lower_ref, sems.at[2]),
            pltpu.make_async_copy(second_hbm, second_ref, sems.at[3]),
            pltpu.make_async_copy(bias_hbm, bias_ref, sems.at[4]),
        ]
        blocks = tiles // many
        locals_, starts = [], []
        for n in range(blocks):
            these, here = pl.ds(n * many, many), pl.ds(n * block, block)
            locals_.append(pltpu.make_async_copy(local_hbm.at[these], local_ref.at[these], in_sems.at[0, n]))
            starts.append(pltpu.make_async_copy(start_hbm.at[here, :], start_ref.at[here, :], in_sems.at[1, n]))
        slot_copy.start()
        halo_copy.start()
        for n in range(blocks):
            locals_[n].start()
            if n == 0:
                for copy in rest:
                    copy.start()
            starts[n].start()
        halo_copy.wait()
        column = lax.broadcasted_iota(I32, (hots, doms * 8), 1)
        ends = halo_ref[:, 2 * cap :, :].reshape(doms * 8, half)
        left = jnp.where(column == at_ref[...], 1.0, 0.0).astype(BF16)
        right = jnp.where(column == at_ref[...] + 4, 1.0, 0.0).astype(BF16)
        drivers = jnp.concatenate([_dot(left, ends).astype(BF16), _dot(right, ends).astype(BF16)], axis=1)
        slot_copy.wait()
        copies = []
        for n in range(blocks):
            locals_[n].wait()
            if n == 0:
                for copy in rest:
                    copy.wait()
            starts[n].wait()
            aggregate = []
            for t in range(n * many, (n + 1) * many):
                which = pl.ds(pl.multiple_of(slot_ref[0, t] * per, per), per)
                halo_tile = jnp.concatenate(
                    [
                        halo_ref[which, :cap, :].reshape(tile, half),
                        halo_ref[which, cap : 2 * cap, :].reshape(tile, half),
                    ],
                    axis=1,
                )
                edges = jnp.concatenate([adj_ref[t, 0], adj_ref[t, 1], dw_ref[t * tile : (t + 1) * tile, :]], axis=1)
                sources = jnp.concatenate([local_ref[t], halo_tile, drivers], axis=0)
                aggregate.append(_dot(edges, sources).astype(BF16))
            here = slice(n * block, (n + 1) * block)
            inner = start_ref[here, :] + _dot(jnp.concatenate(aggregate, axis=0), lower_ref[...])
            activated = (0.5 * inner * (1.0 + lax.erf(inner * (0.5**0.5)))).astype(BF16)
            out[here, :] = (emb_ref[here, :].astype(F32) + bias_ref[...] + _dot(activated, second_ref[...])).astype(
                BF16
            )
            copies.append(pltpu.make_async_copy(out.at[here, :], out_hbm.at[here, :], out_sems.at[n]))
            copies[-1].start()
        for copy in copies:
            copy.wait()

    hbm = pl.BlockSpec(memory_space=pltpu.HBM)
    vmem = pl.BlockSpec(memory_space=pltpu.VMEM)
    return pl.pallas_call(
        body,
        out_shape=jax.ShapeDtypeStruct((rows, width), BF16),
        in_specs=[hbm] * 7 + [vmem] * 4,
        out_specs=hbm,
        scratch_shapes=[
            pltpu.VMEM(halo.shape, BF16),
            pltpu.VMEM(local_tiles.shape, BF16),
            pltpu.VMEM(start.shape, F32),
            pltpu.VMEM(lower.shape, BF16),
            pltpu.VMEM(second.shape, BF16),
            pltpu.SMEM((1, tiles), I32),
            pltpu.VMEM(second_bias.shape, F32),
            pltpu.VMEM((rows, width), BF16),
            pltpu.SemaphoreType.DMA((5,)),
            pltpu.SemaphoreType.DMA((2, tiles // many)),
            pltpu.SemaphoreType.DMA((tiles // many,)),
        ],
        compiler_params=_params(24),
        name="after_halo",
    )(
        *map(_far, (halo, local_tiles, start, lower, second, halo_slot.reshape(1, tiles), second_bias)),
        *map(_near, (driver_at, adjacency, driver_weight, embedding)),
    )


def per_device(
    embedding,
    scenario_feats,
    adjacency,
    driver_weight,
    local_slot,
    halo_slot,
    send_rows,
    send_count,
    hot_ids,
    first_weight,
    feature_weight,
    first_bias,
    second_weight,
    second_bias,
):
    rows, width = embedding.shape
    tile = adjacency.shape[-1]
    tiles = rows // tile
    groups = lax.axis_size("scen")
    myself = lax.axis_index(("dom", "scen")).astype(I32).reshape(1)
    group = lax.axis_index("scen").astype(I32).reshape(1)

    page = note(myself, hot_ids, local_slot, embedding, groups)
    notes = lax.all_to_all(page, "scen", split_axis=0, concat_axis=0, tiled=True)
    message = pick_rows(send_rows, send_count, embedding)
    message = add_drivers(notes, message)
    halo = lax.all_to_all(message, "dom", split_axis=0, concat_axis=0, tiled=True)

    slots = notes[:, 1, :tiles].astype(I32)
    leaving = pick_tiles(group, slots, embedding, first_weight, second_weight, tile)
    arrived = [
        lax.ppermute(x, "scen", [(g, (g + k) % groups) for g in range(groups)])
        for k, x in enumerate(leaving, start=1)
    ]
    local_tiles, start, lower, second = ready(
        group,
        local_slot,
        embedding,
        arrived,
        first_weight,
        second_weight,
        scenario_feats,
        feature_weight,
        first_bias.reshape(1, width),
        tile,
    )
    owner = hot_ids // rows
    driver_at = (owner // groups * 8 + owner % groups).reshape(-1, 1)
    return after_halo(
        halo_slot,
        halo,
        driver_at,
        local_tiles,
        start,
        adjacency,
        driver_weight,
        embedding,
        lower,
        second,
        second_bias.reshape(1, width),
    )


def solution(mesh):
    return jax.shard_map(
        per_device,
        mesh=mesh,
        in_specs=(
            P(("dom", "scen"), None),
            P(None, ("dom", "scen")),
            P(("dom", "scen"), None, None, None),
            P(("dom", "scen"), None),
            P(("dom", "scen")),
            P(("dom", "scen")),
            P(("dom", "scen"), None),
            P(("dom", "scen")),
            P(),
            P("scen", None),
            P(),
            P(),
            P("scen", None),
            P(),
        ),
        out_specs=P(("dom", "scen"), None),
        check_vma=False,
    )
```

```python
import jax
import jax.numpy as jnp
from jax import lax
from jax.experimental import pallas as pl
from jax.experimental.pallas import tpu as pltpu
from jax.sharding import PartitionSpec as P

BF16, F32, I32 = jnp.bfloat16, jnp.float32, jnp.int32
NOTE = 16


def _params(mebibytes):
    return pltpu.CompilerParams(vmem_limit_bytes=mebibytes * 1024 * 1024)


def _near(x):
    return pltpu.with_memory_space_constraint(x, pltpu.VMEM)


def _far(x):
    return pltpu.with_memory_space_constraint(x, pltpu.HBM)


def _dot(a, b):
    return jnp.dot(a, b, preferred_element_type=F32)


def note(myself, hot_ids, local_slot, embedding, groups):
    rows, width = embedding.shape
    hots, tiles = hot_ids.shape[0], local_slot.shape[0]

    def body(myself_ref, hot_hbm, slot_hbm, emb_ref, out_ref, hot_ref, slot_ref, block, page, sems):
        hot_copy = pltpu.make_async_copy(hot_hbm, hot_ref, sems.at[0])
        slot_copy = pltpu.make_async_copy(slot_hbm, slot_ref, sems.at[1])
        hot_copy.start()
        slot_copy.start()
        page[...] = jnp.zeros((NOTE, width), F32)
        hot_copy.wait()
        within = hot_ref[...] - myself_ref[0] * rows
        row = jnp.max(jnp.where((within >= 0) & (within < rows), within, -1))
        start = pl.multiple_of((jnp.maximum(row, 0) // NOTE) * NOTE, NOTE)
        copy = pltpu.make_async_copy(emb_ref.at[pl.ds(start, NOTE), :], block, sems.at[2])
        copy.start()
        slot_copy.wait()
        page[1:2, :tiles] = slot_ref[...].astype(F32)
        copy.wait()
        at = lax.broadcasted_iota(I32, (NOTE, width), 0)
        mine = jnp.where(at == row - start, block[...].astype(F32), 0.0)
        page[0:1, :] = jnp.sum(mine, axis=0, keepdims=True)
        out_ref[...] = jnp.broadcast_to(page[...].astype(BF16)[None], (groups, NOTE, width))

    hbm = pl.BlockSpec(memory_space=pltpu.HBM)
    return pl.pallas_call(
        body,
        out_shape=pltpu.VMEM((groups, NOTE, width), BF16),
        in_specs=[pl.BlockSpec(memory_space=pltpu.SMEM), hbm, hbm, hbm],
        out_specs=pl.BlockSpec(memory_space=pltpu.VMEM),
        scratch_shapes=[
            pltpu.VMEM((1, hots), I32),
            pltpu.VMEM((1, tiles), I32),
            pltpu.VMEM((NOTE, width), BF16),
            pltpu.VMEM((NOTE, width), F32),
            pltpu.SemaphoreType.DMA((3,)),
        ],
        compiler_params=_params(1),
        name="note",
    )(myself, _far(hot_ids.reshape(1, hots)), _far(local_slot.reshape(1, tiles)), _far(embedding))


def pick_rows(send_rows, send_count, embedding):
    rows, width = embedding.shape
    doms, cap = send_rows.shape
    half = width // 2
    step = 32
    parts = rows // 128

    def body(rows_ref, count_ref, emb_ref, out_hbm, out_ref, sems):
        slot = lax.broadcasted_iota(I32, (cap, doms), 0)
        index = jnp.where(slot < count_ref[...], rows_ref[...], -1)
        low = (index & 127).astype(F32)
        high = (index >> 7).astype(F32)
        lane = lax.broadcasted_iota(I32, (cap, 128), 1).astype(F32).astype(BF16)
        one, zero = jnp.ones((), BF16), jnp.zeros((), BF16)
        copies = []
        for i in range(0, doms, step):
            chosen = []
            for p in range(i, i + step):
                low_p = jnp.broadcast_to(low[:, p : p + 1], (cap, 128)).astype(BF16)
                high_p = jnp.broadcast_to(high[:, p : p + 1], (cap, 128)).astype(BF16)
                at = jnp.where(low_p == lane, one, zero)
                chosen.append(
                    jnp.concatenate([jnp.where(high_p == jnp.asarray(k, BF16), at, zero) for k in range(parts)], axis=1)
                )
            got = _dot(jnp.concatenate(chosen, axis=0), emb_ref[...]).astype(BF16).reshape(step, cap, width)
            out_ref[i : i + step, :cap, :] = got[:, :, :half]
            out_ref[i : i + step, cap : 2 * cap, :] = got[:, :, half:]
            copies.append(
                pltpu.make_async_copy(
                    out_ref.at[i : i + step], out_hbm.at[i : i + step, : 2 * cap, :], sems.at[i // step]
                )
            )
            copies[-1].start()
        for copy in copies:
            copy.wait()

    return pl.pallas_call(
        body,
        out_shape=pltpu.HBM((doms, 2 * cap + 8, half), BF16),
        in_specs=[
            pl.BlockSpec((cap, doms), lambda: (0, 0)),
            pl.BlockSpec((1, doms), lambda: (0, 0)),
            pl.BlockSpec((rows, width), lambda: (0, 0)),
        ],
        out_specs=pl.BlockSpec(memory_space=pl.ANY),
        scratch_shapes=[pltpu.VMEM((doms, 2 * cap, half), BF16), pltpu.SemaphoreType.DMA((doms // step,))],
        compiler_params=_params(24),
        name="pick_rows",
    )(_near(send_rows.T), _near(send_count.reshape(1, doms)), _near(embedding))


def add_drivers(notes, message):
    doms, length, half = message.shape
    groups = notes.shape[0]

    def body(notes_ref, _, out_ref, page, sem):
        at = lax.broadcasted_iota(I32, (8, half), 0)
        last = jnp.zeros((8, half), F32)
        for g in range(groups):
            row = notes_ref[g].astype(F32)[0:1, :]
            last = jnp.where(at == g, row[:, :half], last)
            last = jnp.where(at == groups + g, row[:, half:], last)
        page[...] = jnp.broadcast_to(last[None], (doms, 8, half)).astype(BF16)
        copy = pltpu.make_async_copy(page, out_ref.at[:, pl.ds(length - 8, 8), :], sem)
        copy.start()
        copy.wait()

    return pl.pallas_call(
        body,
        out_shape=jax.ShapeDtypeStruct(message.shape, BF16),
        in_specs=[pl.BlockSpec(notes.shape, lambda: (0, 0, 0)), pl.BlockSpec(memory_space=pl.ANY)],
        out_specs=pl.BlockSpec(memory_space=pl.ANY),
        scratch_shapes=[pltpu.VMEM((doms, 8, half), BF16), pltpu.SemaphoreType.DMA(())],
        input_output_aliases={1: 0},
        compiler_params=_params(2),
        name="add_drivers",
    )(notes, _far(message))


def pick_tiles(group, slots, embedding, first_weight, second_weight, tile):
    groups, tiles = slots.shape
    rows, width = embedding.shape
    each = tiles // groups
    a, b = first_weight.shape[0], second_weight.shape[0]
    length = each * tile + a + b

    def body(group_ref, slots_ref, emb_ref, first_ref, second_ref, *rest):
        outs, (listed, sems) = rest[: groups - 1], rest[groups - 1 :]
        me = group_ref[0]
        copies = []
        for k in range(1, groups):
            out = outs[k - 1]
            other = (me + k) % groups
            copies.append(pltpu.make_async_copy(first_ref, out.at[pl.ds(each * tile, a), :], sems.at[k - 1, each]))
            copies.append(
                pltpu.make_async_copy(second_ref, out.at[pl.ds(each * tile + a, b), :], sems.at[k - 1, each + 1])
            )
            for j in range(each):
                listed[k - 1, j] = 0

            def look(t, found, k=k, other=other):
                tile_at = slots_ref[other, t]
                hit = tile_at // tiles == me

                @pl.when(hit)
                def _():
                    listed[k - 1, jnp.minimum(found, each - 1)] = tile_at - me * tiles

                return found + hit.astype(I32)

            lax.fori_loop(0, tiles, look, jnp.zeros((), I32))
            for j in range(each):
                start = pl.multiple_of(listed[k - 1, j] * tile, tile)
                copies.append(
                    pltpu.make_async_copy(
                        emb_ref.at[pl.ds(start, tile), :], out.at[pl.ds(j * tile, tile), :], sems.at[k - 1, j]
                    )
                )
        for copy in copies:
            copy.start()
        for copy in copies:
            copy.wait()

    hbm = pl.BlockSpec(memory_space=pl.ANY)
    smem = pl.BlockSpec(memory_space=pltpu.SMEM)
    return pl.pallas_call(
        body,
        out_shape=[pltpu.HBM((length, width), BF16)] * (groups - 1),
        in_specs=[smem, smem, hbm, hbm, hbm],
        out_specs=[hbm] * (groups - 1),
        scratch_shapes=[
            pltpu.SMEM((groups - 1, each), I32),
            pltpu.SemaphoreType.DMA((groups - 1, each + 2)),
        ],
        compiler_params=_params(2),
        name="pick_tiles",
    )(group, slots, _near(embedding), first_weight, second_weight)


def ready(
    group, slot, embedding, arrived, first_weight, second_weight, feats, feature_weight, first_bias, tile
):
    rows, width = embedding.shape
    tiles = slot.shape[0]
    groups = len(arrived) + 1
    each = tiles // groups
    a, b = first_weight.shape[0], second_weight.shape[0]
    many = rows // 4

    def body(group_ref, slot_ref, emb_ref, own_a, own_b, feat_hbm, fw_hbm, bias_hbm, *rest):
        parts = rest[: groups - 1]
        tiles_hbm, start_hbm, lower_ref, second_hbm, *rest = rest[groups - 1 :]
        tiles_ref, start_ref, weight, second_ref, feat_ref, fw_ref, bias_ref, tile_sems, start_sems, sems, small_sems = rest
        me = group_ref[0]
        small = [
            pltpu.make_async_copy(feat_hbm, feat_ref, small_sems.at[0]),
            pltpu.make_async_copy(fw_hbm, fw_ref, small_sems.at[1]),
            pltpu.make_async_copy(bias_hbm, bias_ref, small_sems.at[2]),
        ]
        firsts, seconds = [], []
        for k in range(groups):
            other = (me + groups - k) % groups
            from_a = own_a if k == 0 else parts[k - 1].at[pl.ds(each * tile, a), :]
            from_b = own_b if k == 0 else parts[k - 1].at[pl.ds(each * tile + a, b), :]
            to_a = weight.at[pl.ds(pl.multiple_of(other * a, a), a), :]
            to_b = second_ref.at[pl.ds(pl.multiple_of(other * b, b), b), :]
            firsts.append(pltpu.make_async_copy(from_a, to_a, sems.at[0, k]))
            seconds.append(pltpu.make_async_copy(from_b, to_b, sems.at[1, k]))
        for copy in (*firsts, *small, *seconds):
            copy.start()

        def send(t, counts):
            source = slot_ref[t] // tiles
            spot = sum(jnp.where(source == g, counts[g], 0) for g in range(groups))
            away = (me + groups - source) % groups
            for k in range(groups):

                @pl.when(away == k)
                def _(k=k):
                    if k == 0:
                        at = pl.multiple_of((slot_ref[t] - source * tiles) * tile, tile)
                        copy = pltpu.make_async_copy(emb_ref.at[pl.ds(at, tile), :], tiles_ref.at[t], tile_sems.at[t])
                    else:
                        at = pl.multiple_of(jnp.minimum(spot, each - 1) * tile, tile)
                        here = parts[k - 1].at[pl.ds(at, tile), :]
                        copy = pltpu.make_async_copy(here, tiles_ref.at[t], tile_sems.at[t])
                    copy.start()

            return tuple(counts[g] + (source == g).astype(I32) for g in range(groups))

        lax.fori_loop(0, tiles, send, (jnp.zeros((), I32),) * groups)
        for copy in (*firsts, *small):
            copy.wait()
        leaving = [pltpu.make_async_copy(weight.at[pl.ds(width, width), :], lower_ref, small_sems.at[0])]
        leaving[0].start()
        for n in range(rows // many):
            here = pl.ds(n * many, many)
            start_ref[here, :] = (
                _dot(emb_ref[here, :], weight[:width, :])
                + lax.dot_general(
                    feat_ref[:, n * many : (n + 1) * many],
                    fw_ref[...],
                    (((0,), (0,)), ((), ())),
                    preferred_element_type=F32,
                )
                + bias_ref[...]
            )
            leaving.append(pltpu.make_async_copy(start_ref.at[here, :], start_hbm.at[here, :], start_sems.at[n]))
            leaving[-1].start()
        for t in range(tiles):
            pltpu.make_async_copy(emb_ref.at[pl.ds(0, tile), :], tiles_ref.at[t], tile_sems.at[t]).wait()
        leaving.append(pltpu.make_async_copy(tiles_ref, tiles_hbm, small_sems.at[1]))
        leaving[-1].start()
        for copy in seconds:
            copy.wait()
        leaving.append(pltpu.make_async_copy(second_ref, second_hbm, small_sems.at[2]))
        leaving[-1].start()
        for copy in leaving:
            copy.wait()

    smem = pl.BlockSpec(memory_space=pltpu.SMEM)
    hbm = pl.BlockSpec(memory_space=pltpu.HBM)
    return pl.pallas_call(
        body,
        out_shape=[
            pltpu.HBM((tiles, tile, width), BF16),
            pltpu.HBM((rows, width), F32),
            pltpu.HBM((width, width), BF16),
            pltpu.HBM((width, width), BF16),
        ],
        in_specs=[smem, smem, pl.BlockSpec(memory_space=pltpu.VMEM)] + [hbm] * (5 + len(arrived)),
        out_specs=[hbm] * 4,
        scratch_shapes=[
            pltpu.VMEM((tiles, tile, width), BF16),
            pltpu.VMEM((rows, width), F32),
            pltpu.VMEM((2 * width, width), BF16),
            pltpu.VMEM((width, width), BF16),
            pltpu.VMEM(feats.shape, BF16),
            pltpu.VMEM(feature_weight.shape, BF16),
            pltpu.VMEM(first_bias.shape, F32),
            pltpu.SemaphoreType.DMA((tiles,)),
            pltpu.SemaphoreType.DMA((rows // many,)),
            pltpu.SemaphoreType.DMA((2, groups)),
            pltpu.SemaphoreType.DMA((3,)),
        ],
        compiler_params=_params(12),
        name="ready",
    )(
        group,
        slot,
        _near(embedding),
        *map(_far, (first_weight, second_weight, feats, feature_weight, first_bias, *arrived)),
    )


def after_halo(
    halo_slot, halo, driver_at, local_tiles, start, adjacency, driver_weight, embedding, lower, second, second_bias
):
    rows, width = embedding.shape
    tiles, _, tile, _ = adjacency.shape
    doms, length, half = halo.shape
    cap = (length - 8) // 2
    hots = driver_weight.shape[1]
    many = tiles // 4
    block = many * tile
    per = tile // cap

    def body(
        halo_hbm, local_hbm, start_hbm, lower_hbm, second_hbm, slot_hbm, bias_hbm, at_ref, adj_ref, dw_ref, emb_ref,
        out_hbm, halo_ref, local_ref, start_ref, lower_ref, second_ref, slot_ref, bias_ref, out, sems, in_sems, out_sems,
    ):
        halo_copy = pltpu.make_async_copy(halo_hbm, halo_ref, sems.at[0])
        slot_copy = pltpu.make_async_copy(slot_hbm, slot_ref, sems.at[1])
        rest = [
            pltpu.make_async_copy(lower_hbm, lower_ref, sems.at[2]),
            pltpu.make_async_copy(second_hbm, second_ref, sems.at[3]),
            pltpu.make_async_copy(bias_hbm, bias_ref, sems.at[4]),
        ]
        blocks = tiles // many
        locals_, starts = [], []
        for n in range(blocks):
            these, here = pl.ds(n * many, many), pl.ds(n * block, block)
            locals_.append(pltpu.make_async_copy(local_hbm.at[these], local_ref.at[these], in_sems.at[0, n]))
            starts.append(pltpu.make_async_copy(start_hbm.at[here, :], start_ref.at[here, :], in_sems.at[1, n]))
        slot_copy.start()
        halo_copy.start()
        for n in range(blocks):
            locals_[n].start()
            if n == 0:
                for copy in rest:
                    copy.start()
            starts[n].start()
        halo_copy.wait()
        column = lax.broadcasted_iota(I32, (hots, doms * 8), 1)
        ends = halo_ref[:, 2 * cap :, :].reshape(doms * 8, half)
        left = jnp.where(column == at_ref[...], 1.0, 0.0).astype(BF16)
        right = jnp.where(column == at_ref[...] + 4, 1.0, 0.0).astype(BF16)
        drivers = jnp.concatenate([_dot(left, ends).astype(BF16), _dot(right, ends).astype(BF16)], axis=1)
        slot_copy.wait()
        copies = []
        for n in range(blocks):
            locals_[n].wait()
            if n == 0:
                for copy in rest:
                    copy.wait()
            starts[n].wait()
            aggregate = []
            for t in range(n * many, (n + 1) * many):
                which = pl.ds(pl.multiple_of(slot_ref[0, t] * per, per), per)
                halo_tile = jnp.concatenate(
                    [
                        halo_ref[which, :cap, :].reshape(tile, half),
                        halo_ref[which, cap : 2 * cap, :].reshape(tile, half),
                    ],
                    axis=1,
                )
                edges = jnp.concatenate([adj_ref[t, 0], adj_ref[t, 1], dw_ref[t * tile : (t + 1) * tile, :]], axis=1)
                sources = jnp.concatenate([local_ref[t], halo_tile, drivers], axis=0)
                aggregate.append(_dot(edges, sources).astype(BF16))
            here = slice(n * block, (n + 1) * block)
            inner = start_ref[here, :] + _dot(jnp.concatenate(aggregate, axis=0), lower_ref[...])
            activated = (0.5 * inner * (1.0 + lax.erf(inner * (0.5**0.5)))).astype(BF16)
            out[here, :] = (emb_ref[here, :].astype(F32) + bias_ref[...] + _dot(activated, second_ref[...])).astype(
                BF16
            )
            copies.append(pltpu.make_async_copy(out.at[here, :], out_hbm.at[here, :], out_sems.at[n]))
            copies[-1].start()
        for copy in copies:
            copy.wait()

    hbm = pl.BlockSpec(memory_space=pltpu.HBM)
    vmem = pl.BlockSpec(memory_space=pltpu.VMEM)
    return pl.pallas_call(
        body,
        out_shape=jax.ShapeDtypeStruct((rows, width), BF16),
        in_specs=[hbm] * 7 + [vmem] * 4,
        out_specs=hbm,
        scratch_shapes=[
            pltpu.VMEM(halo.shape, BF16),
            pltpu.VMEM(local_tiles.shape, BF16),
            pltpu.VMEM(start.shape, F32),
            pltpu.VMEM(lower.shape, BF16),
            pltpu.VMEM(second.shape, BF16),
            pltpu.SMEM((1, tiles), I32),
            pltpu.VMEM(second_bias.shape, F32),
            pltpu.VMEM((rows, width), BF16),
            pltpu.SemaphoreType.DMA((5,)),
            pltpu.SemaphoreType.DMA((2, tiles // many)),
            pltpu.SemaphoreType.DMA((tiles // many,)),
        ],
        compiler_params=_params(24),
        name="after_halo",
    )(
        *map(_far, (halo, local_tiles, start, lower, second, halo_slot.reshape(1, tiles), second_bias)),
        *map(_near, (driver_at, adjacency, driver_weight, embedding)),
    )


def per_device(
    embedding,
    scenario_feats,
    adjacency,
    driver_weight,
    local_slot,
    halo_slot,
    send_rows,
    send_count,
    hot_ids,
    first_weight,
    feature_weight,
    first_bias,
    second_weight,
    second_bias,
):
    rows, width = embedding.shape
    tile = adjacency.shape[-1]
    tiles = rows // tile
    groups = lax.axis_size("scen")
    myself = lax.axis_index(("dom", "scen")).astype(I32).reshape(1)
    group = lax.axis_index("scen").astype(I32).reshape(1)

    page = note(myself, hot_ids, local_slot, embedding, groups)
    notes = lax.all_to_all(page, "scen", split_axis=0, concat_axis=0, tiled=True)
    message = pick_rows(send_rows, send_count, embedding)
    message = add_drivers(notes, message)
    halo = lax.all_to_all(message, "dom", split_axis=0, concat_axis=0, tiled=True)

    slots = notes[:, 1, :tiles].astype(I32)
    leaving = pick_tiles(group, slots, embedding, first_weight, second_weight, tile)
    arrived = [
        lax.ppermute(x, "scen", [(g, (g + k) % groups) for g in range(groups)])
        for k, x in enumerate(leaving, start=1)
    ]
    local_tiles, start, lower, second = ready(
        group,
        local_slot,
        embedding,
        arrived,
        first_weight,
        second_weight,
        scenario_feats,
        feature_weight,
        first_bias.reshape(1, width),
        tile,
    )
    owner = hot_ids // rows
    driver_at = (owner // groups * 8 + owner % groups).reshape(-1, 1)
    return after_halo(
        halo_slot,
        halo,
        driver_at,
        local_tiles,
        start,
        adjacency,
        driver_weight,
        embedding,
        lower,
        second,
        second_bias.reshape(1, width),
    )


def solution(mesh):
    return jax.shard_map(
        per_device,
        mesh=mesh,
        in_specs=(
            P(("dom", "scen"), None),
            P(None, ("dom", "scen")),
            P(("dom", "scen"), None, None, None),
            P(("dom", "scen"), None),
            P(("dom", "scen")),
            P(("dom", "scen")),
            P(("dom", "scen"), None),
            P(("dom", "scen")),
            P(),
            P("scen", None),
            P(),
            P(),
            P("scen", None),
            P(),
        ),
        out_specs=P(("dom", "scen"), None),
        check_vma=False,
    )
```

```python
import jax
import jax.numpy as jnp
from jax import lax
from jax.experimental import pallas as pl
from jax.experimental.pallas import tpu as pltpu
from jax.sharding import PartitionSpec as P

BF16, F32, I32 = jnp.bfloat16, jnp.float32, jnp.int32
NOTE = 16


def _params(mebibytes):
    return pltpu.CompilerParams(vmem_limit_bytes=mebibytes * 1024 * 1024)


def _near(x):
    return pltpu.with_memory_space_constraint(x, pltpu.VMEM)


def _far(x):
    return pltpu.with_memory_space_constraint(x, pltpu.HBM)


def _dot(a, b):
    return jnp.dot(a, b, preferred_element_type=F32)


def note(myself, hot_ids, local_slot, embedding, groups):
    rows, width = embedding.shape
    hots, tiles = hot_ids.shape[0], local_slot.shape[0]

    def body(myself_ref, hot_hbm, slot_hbm, emb_ref, out_ref, hot_ref, slot_ref, block, page, sems):
        hot_copy = pltpu.make_async_copy(hot_hbm, hot_ref, sems.at[0])
        slot_copy = pltpu.make_async_copy(slot_hbm, slot_ref, sems.at[1])
        hot_copy.start()
        slot_copy.start()
        page[...] = jnp.zeros((NOTE, width), F32)
        hot_copy.wait()
        within = hot_ref[...] - myself_ref[0] * rows
        row = jnp.max(jnp.where((within >= 0) & (within < rows), within, -1))
        start = pl.multiple_of((jnp.maximum(row, 0) // NOTE) * NOTE, NOTE)
        copy = pltpu.make_async_copy(emb_ref.at[pl.ds(start, NOTE), :], block, sems.at[2])
        copy.start()
        slot_copy.wait()
        page[1:2, :tiles] = slot_ref[...].astype(F32)
        copy.wait()
        at = lax.broadcasted_iota(I32, (NOTE, width), 0)
        mine = jnp.where(at == row - start, block[...].astype(F32), 0.0)
        page[0:1, :] = jnp.sum(mine, axis=0, keepdims=True)
        out_ref[...] = jnp.broadcast_to(page[...].astype(BF16)[None], (groups, NOTE, width))

    hbm = pl.BlockSpec(memory_space=pltpu.HBM)
    return pl.pallas_call(
        body,
        out_shape=pltpu.VMEM((groups, NOTE, width), BF16),
        in_specs=[pl.BlockSpec(memory_space=pltpu.SMEM), hbm, hbm, hbm],
        out_specs=pl.BlockSpec(memory_space=pltpu.VMEM),
        scratch_shapes=[
            pltpu.VMEM((1, hots), I32),
            pltpu.VMEM((1, tiles), I32),
            pltpu.VMEM((NOTE, width), BF16),
            pltpu.VMEM((NOTE, width), F32),
            pltpu.SemaphoreType.DMA((3,)),
        ],
        compiler_params=_params(1),
        name="note",
    )(myself, _far(hot_ids.reshape(1, hots)), _far(local_slot.reshape(1, tiles)), _far(embedding))


def pick_rows(send_rows, send_count, embedding):
    rows, width = embedding.shape
    doms, cap = send_rows.shape
    half = width // 2
    step = 32
    parts = rows // 128

    def body(rows_ref, count_ref, emb_ref, out_hbm, out_ref, sems):
        slot = lax.broadcasted_iota(I32, (cap, doms), 0)
        index = jnp.where(slot < count_ref[...], rows_ref[...], -1)
        low = (index & 127).astype(F32)
        high = (index >> 7).astype(F32)
        lane = lax.broadcasted_iota(I32, (cap, 128), 1).astype(F32).astype(BF16)
        one, zero = jnp.ones((), BF16), jnp.zeros((), BF16)
        copies = []
        for i in range(0, doms, step):
            chosen = []
            for p in range(i, i + step):
                low_p = jnp.broadcast_to(low[:, p : p + 1], (cap, 128)).astype(BF16)
                high_p = jnp.broadcast_to(high[:, p : p + 1], (cap, 128)).astype(BF16)
                at = jnp.where(low_p == lane, one, zero)
                chosen.append(
                    jnp.concatenate([jnp.where(high_p == jnp.asarray(k, BF16), at, zero) for k in range(parts)], axis=1)
                )
            got = _dot(jnp.concatenate(chosen, axis=0), emb_ref[...]).astype(BF16).reshape(step, cap, width)
            out_ref[i : i + step, :cap, :] = got[:, :, :half]
            out_ref[i : i + step, cap : 2 * cap, :] = got[:, :, half:]
            copies.append(
                pltpu.make_async_copy(
                    out_ref.at[i : i + step], out_hbm.at[i : i + step, : 2 * cap, :], sems.at[i // step]
                )
            )
            copies[-1].start()
        for copy in copies:
            copy.wait()

    return pl.pallas_call(
        body,
        out_shape=pltpu.HBM((doms, 2 * cap + 8, half), BF16),
        in_specs=[
            pl.BlockSpec((cap, doms), lambda: (0, 0)),
            pl.BlockSpec((1, doms), lambda: (0, 0)),
            pl.BlockSpec((rows, width), lambda: (0, 0)),
        ],
        out_specs=pl.BlockSpec(memory_space=pl.ANY),
        scratch_shapes=[pltpu.VMEM((doms, 2 * cap, half), BF16), pltpu.SemaphoreType.DMA((doms // step,))],
        compiler_params=_params(24),
        name="pick_rows",
    )(_near(send_rows.T), _near(send_count.reshape(1, doms)), _near(embedding))


def add_drivers(notes, message):
    doms, length, half = message.shape
    groups = notes.shape[0]

    def body(notes_ref, _, out_ref, page, sem):
        at = lax.broadcasted_iota(I32, (8, half), 0)
        last = jnp.zeros((8, half), F32)
        for g in range(groups):
            row = notes_ref[g].astype(F32)[0:1, :]
            last = jnp.where(at == g, row[:, :half], last)
            last = jnp.where(at == groups + g, row[:, half:], last)
        page[...] = jnp.broadcast_to(last[None], (doms, 8, half)).astype(BF16)
        copy = pltpu.make_async_copy(page, out_ref.at[:, pl.ds(length - 8, 8), :], sem)
        copy.start()
        copy.wait()

    return pl.pallas_call(
        body,
        out_shape=jax.ShapeDtypeStruct(message.shape, BF16),
        in_specs=[pl.BlockSpec(notes.shape, lambda: (0, 0, 0)), pl.BlockSpec(memory_space=pl.ANY)],
        out_specs=pl.BlockSpec(memory_space=pl.ANY),
        scratch_shapes=[pltpu.VMEM((doms, 8, half), BF16), pltpu.SemaphoreType.DMA(())],
        input_output_aliases={1: 0},
        compiler_params=_params(2),
        name="add_drivers",
    )(notes, _far(message))


def pick_tiles(group, slots, embedding, first_weight, second_weight, tile):
    groups, tiles = slots.shape
    rows, width = embedding.shape
    each = tiles // groups
    a, b = first_weight.shape[0], second_weight.shape[0]
    length = each * tile + a + b

    def body(group_ref, slots_ref, emb_ref, first_ref, second_ref, *rest):
        outs, (listed, sems) = rest[: groups - 1], rest[groups - 1 :]
        me = group_ref[0]
        copies = []
        for k in range(1, groups):
            out = outs[k - 1]
            other = (me + k) % groups
            copies.append(pltpu.make_async_copy(first_ref, out.at[pl.ds(each * tile, a), :], sems.at[k - 1, each]))
            copies.append(
                pltpu.make_async_copy(second_ref, out.at[pl.ds(each * tile + a, b), :], sems.at[k - 1, each + 1])
            )
            for j in range(each):
                listed[k - 1, j] = 0

            def look(t, found, k=k, other=other):
                tile_at = slots_ref[other, t]
                hit = (tile_at >= me * tiles) & (tile_at < (me + 1) * tiles)

                @pl.when(hit)
                def _():
                    listed[k - 1, jnp.minimum(found, each - 1)] = tile_at - me * tiles

                return found + hit.astype(I32)

            lax.fori_loop(0, tiles, look, jnp.zeros((), I32))
            for j in range(each):
                start = pl.multiple_of(listed[k - 1, j] * tile, tile)
                copies.append(
                    pltpu.make_async_copy(
                        emb_ref.at[pl.ds(start, tile), :], out.at[pl.ds(j * tile, tile), :], sems.at[k - 1, j]
                    )
                )
        for copy in copies:
            copy.start()
        for copy in copies:
            copy.wait()

    hbm = pl.BlockSpec(memory_space=pl.ANY)
    smem = pl.BlockSpec(memory_space=pltpu.SMEM)
    return pl.pallas_call(
        body,
        out_shape=[pltpu.HBM((length, width), BF16)] * (groups - 1),
        in_specs=[smem, smem, hbm, hbm, hbm],
        out_specs=[hbm] * (groups - 1),
        scratch_shapes=[
            pltpu.SMEM((groups - 1, each), I32),
            pltpu.SemaphoreType.DMA((groups - 1, each + 2)),
        ],
        compiler_params=_params(2),
        name="pick_tiles",
    )(group, slots, _near(embedding), first_weight, second_weight)


def ready(group, slot, embedding, arrived, first_weight, second_weight, tile):
    width = embedding.shape[1]
    tiles = slot.shape[0]
    groups = len(arrived) + 1
    each = tiles // groups
    a, b = first_weight.shape[0], second_weight.shape[0]

    def body(group_ref, slot_ref, emb_ref, own_a, own_b, *rest):
        parts = rest[: groups - 1]
        tiles_hbm, first_hbm, second_hbm, tiles_ref, first_ref, second_ref, tile_sems, sems, out_sems = rest[groups - 1 :]
        me = group_ref[0]
        firsts, seconds = [], []
        for k in range(groups):
            other = (me + groups - k) % groups
            from_a = own_a if k == 0 else parts[k - 1].at[pl.ds(each * tile, a), :]
            from_b = own_b if k == 0 else parts[k - 1].at[pl.ds(each * tile + a, b), :]
            to_a = first_ref.at[pl.ds(pl.multiple_of(other * a, a), a), :]
            to_b = second_ref.at[pl.ds(pl.multiple_of(other * b, b), b), :]
            firsts.append(pltpu.make_async_copy(from_a, to_a, sems.at[0, k]))
            seconds.append(pltpu.make_async_copy(from_b, to_b, sems.at[1, k]))

        def send(t, counts):
            tile_at = slot_ref[t]
            source = sum((tile_at >= tiles * g).astype(I32) for g in range(1, groups))
            spot = sum(jnp.where(source == g, counts[g], 0) for g in range(groups))
            away = (me + groups - source) % groups
            for k in range(groups):

                @pl.when(away == k)
                def _(k=k):
                    if k == 0:
                        at = pl.multiple_of((tile_at - source * tiles) * tile, tile)
                        here = emb_ref.at[pl.ds(at, tile), :]
                    else:
                        at = pl.multiple_of(jnp.minimum(spot, each - 1) * tile, tile)
                        here = parts[k - 1].at[pl.ds(at, tile), :]
                    pltpu.make_async_copy(here, tiles_ref.at[t], tile_sems.at[t]).start()

            return tuple(counts[g] + (source == g).astype(I32) for g in range(groups))

        lax.fori_loop(0, tiles, send, (jnp.zeros((), I32),) * groups)
        for copy in (*firsts, *seconds):
            copy.start()
        for t in range(tiles):
            pltpu.make_async_copy(emb_ref.at[pl.ds(0, tile), :], tiles_ref.at[t], tile_sems.at[t]).wait()
        leaving = [pltpu.make_async_copy(tiles_ref, tiles_hbm, out_sems.at[0])]
        leaving[-1].start()
        for n, (copies, here, there) in enumerate(
            ((firsts, first_ref, first_hbm), (seconds, second_ref, second_hbm)), start=1
        ):
            for copy in copies:
                copy.wait()
            leaving.append(pltpu.make_async_copy(here, there, out_sems.at[n]))
            leaving[-1].start()
        for copy in leaving:
            copy.wait()

    smem = pl.BlockSpec(memory_space=pltpu.SMEM)
    hbm = pl.BlockSpec(memory_space=pltpu.HBM)
    return pl.pallas_call(
        body,
        out_shape=[
            pltpu.HBM((tiles, tile, width), BF16),
            pltpu.HBM((groups * a, width), BF16),
            pltpu.HBM((groups * b, width), BF16),
        ],
        in_specs=[smem, smem, pl.BlockSpec(memory_space=pltpu.VMEM)] + [hbm] * (2 + len(arrived)),
        out_specs=[hbm] * 3,
        scratch_shapes=[
            pltpu.VMEM((tiles, tile, width), BF16),
            pltpu.VMEM((groups * a, width), BF16),
            pltpu.VMEM((groups * b, width), BF16),
            pltpu.SemaphoreType.DMA((tiles,)),
            pltpu.SemaphoreType.DMA((2, groups)),
            pltpu.SemaphoreType.DMA((3,)),
        ],
        compiler_params=_params(4),
        name="ready",
    )(group, slot, _near(embedding), *map(_far, (first_weight, second_weight, *arrived)))


def after_halo(
    halo_slot, halo, driver_at, local_tiles, adjacency, driver_weight, embedding, first, second, feats, feature_weight,
    first_bias, second_bias,
):
    rows, width = embedding.shape
    tiles, _, tile, _ = adjacency.shape
    doms, length, half = halo.shape
    cap = (length - 8) // 2
    hots = driver_weight.shape[1]
    many = tiles // 2
    block = many * tile
    per = tile // cap

    def body(local_hbm, adj_hbm, *rest):
        small_hbm, rest = rest[:7], rest[7:]
        halo_ref, at_ref, dw_ref, emb_ref, out_hbm, local_ref, adj_ref, *rest = rest
        small, (out, sems, in_sems, out_sems) = rest[:7], rest[7:]
        slot_ref, first_ref, feat_ref, fw_ref, first_bias_ref, second_ref, second_bias_ref = small
        blocks = tiles // many
        smalls = [pltpu.make_async_copy(x, y, sems.at[n]) for n, (x, y) in enumerate(zip(small_hbm, small))]
        smalls[0].start()
        arriving = []
        for n in range(blocks):
            these = pl.ds(n * many, many)
            arriving.append(
                (
                    pltpu.make_async_copy(local_hbm.at[these], local_ref.at[these], in_sems.at[0, n]),
                    pltpu.make_async_copy(adj_hbm.at[these], adj_ref.at[these], in_sems.at[1, n]),
                )
            )
            for copy in arriving[-1]:
                copy.start()
            if n == 0:
                for copy in smalls[1:]:
                    copy.start()
        column = lax.broadcasted_iota(I32, (hots, doms * 8), 1)
        ends = halo_ref[:, 2 * cap :, :].reshape(doms * 8, half)
        left = jnp.where(column == at_ref[...], 1.0, 0.0).astype(BF16)
        right = jnp.where(column == at_ref[...] + 4, 1.0, 0.0).astype(BF16)
        drivers = jnp.concatenate([_dot(left, ends).astype(BF16), _dot(right, ends).astype(BF16)], axis=1)
        smalls[0].wait()
        copies = []
        for n in range(blocks):
            for copy in arriving[n]:
                copy.wait()
            aggregate = []
            for t in range(n * many, (n + 1) * many):
                which = pl.ds(pl.multiple_of(slot_ref[0, t] * per, per), per)
                halo_tile = jnp.concatenate(
                    [
                        halo_ref[which, :cap, :].reshape(tile, half),
                        halo_ref[which, cap : 2 * cap, :].reshape(tile, half),
                    ],
                    axis=1,
                )
                edges = jnp.concatenate([adj_ref[t, 0], adj_ref[t, 1], dw_ref[t * tile : (t + 1) * tile, :]], axis=1)
                sources = jnp.concatenate([local_ref[t], halo_tile, drivers], axis=0)
                aggregate.append(_dot(edges, sources).astype(BF16))
            if n == 0:
                for copy in smalls[1:]:
                    copy.wait()
            here = slice(n * block, (n + 1) * block)
            own = emb_ref[here, :]
            inner = (
                _dot(jnp.concatenate([own, jnp.concatenate(aggregate, axis=0)], axis=1), first_ref[...])
                + lax.dot_general(
                    feat_ref[:, here], fw_ref[...], (((0,), (0,)), ((), ())), preferred_element_type=F32
                )
                + first_bias_ref[...]
            )
            activated = (0.5 * inner * (1.0 + lax.erf(inner * (0.5**0.5)))).astype(BF16)
            out[here, :] = (own.astype(F32) + second_bias_ref[...] + _dot(activated, second_ref[...])).astype(BF16)
            copies.append(pltpu.make_async_copy(out.at[here, :], out_hbm.at[here, :], out_sems.at[n]))
            copies[-1].start()
        for copy in copies:
            copy.wait()

    hbm = pl.BlockSpec(memory_space=pltpu.HBM)
    vmem = pl.BlockSpec(memory_space=pltpu.VMEM)
    smalls = (halo_slot.reshape(1, tiles), first, feats, feature_weight, first_bias, second, second_bias)
    return pl.pallas_call(
        body,
        out_shape=jax.ShapeDtypeStruct((rows, width), BF16),
        in_specs=[hbm] * 9 + [vmem] * 4,
        out_specs=hbm,
        scratch_shapes=[
            pltpu.VMEM(local_tiles.shape, BF16),
            pltpu.VMEM(adjacency.shape, BF16),
            pltpu.SMEM((1, tiles), I32),
            *[pltpu.VMEM(x.shape, x.dtype) for x in smalls[1:]],
            pltpu.VMEM((rows, width), BF16),
            pltpu.SemaphoreType.DMA((7,)),
            pltpu.SemaphoreType.DMA((2, tiles // many)),
            pltpu.SemaphoreType.DMA((tiles // many,)),
        ],
        compiler_params=_params(24),
        name="after_halo",
    )(
        *map(_far, (local_tiles, adjacency, *smalls)),
        *map(_near, (halo, driver_at, driver_weight, embedding)),
    )


def per_device(
    embedding,
    scenario_feats,
    adjacency,
    driver_weight,
    local_slot,
    halo_slot,
    send_rows,
    send_count,
    hot_ids,
    first_weight,
    feature_weight,
    first_bias,
    second_weight,
    second_bias,
):
    rows, width = embedding.shape
    tile = adjacency.shape[-1]
    tiles = rows // tile
    groups = lax.axis_size("scen")
    myself = lax.axis_index(("dom", "scen")).astype(I32).reshape(1)
    group = lax.axis_index("scen").astype(I32).reshape(1)

    page = note(myself, hot_ids, local_slot, embedding, groups)
    notes = lax.all_to_all(page, "scen", split_axis=0, concat_axis=0, tiled=True)
    message = pick_rows(send_rows, send_count, embedding)
    message = add_drivers(notes, message)
    halo = lax.all_to_all(message, "dom", split_axis=0, concat_axis=0, tiled=True)

    slots = notes[:, 1, :tiles].astype(I32)
    leaving = pick_tiles(group, slots, embedding, first_weight, second_weight, tile)
    arrived = [
        lax.ppermute(x, "scen", [(g, (g + k) % groups) for g in range(groups)])
        for k, x in enumerate(leaving, start=1)
    ]
    local_tiles, first, second = ready(group, local_slot, embedding, arrived, first_weight, second_weight, tile)
    owner = hot_ids // rows
    driver_at = (owner // groups * 8 + owner % groups).reshape(-1, 1)
    return after_halo(
        halo_slot,
        halo,
        driver_at,
        local_tiles,
        adjacency,
        driver_weight,
        embedding,
        first,
        second,
        scenario_feats,
        feature_weight,
        first_bias.reshape(1, width),
        second_bias.reshape(1, width),
    )


def solution(mesh):
    return jax.shard_map(
        per_device,
        mesh=mesh,
        in_specs=(
            P(("dom", "scen"), None),
            P(None, ("dom", "scen")),
            P(("dom", "scen"), None, None, None),
            P(("dom", "scen"), None),
            P(("dom", "scen")),
            P(("dom", "scen")),
            P(("dom", "scen"), None),
            P(("dom", "scen")),
            P(),
            P("scen", None),
            P(),
            P(),
            P("scen", None),
            P(),
        ),
        out_specs=P(("dom", "scen"), None),
        check_vma=False,
    )
```

```python
import jax
import jax.numpy as jnp
from jax import lax
from jax.experimental import pallas as pl
from jax.experimental.pallas import tpu as pltpu
from jax.sharding import PartitionSpec as P

BF16, F32, I32 = jnp.bfloat16, jnp.float32, jnp.int32
NOTE = 16


def _params(mebibytes):
    return pltpu.CompilerParams(vmem_limit_bytes=mebibytes * 1024 * 1024)


def _near(x):
    return pltpu.with_memory_space_constraint(x, pltpu.VMEM)


def _far(x):
    return pltpu.with_memory_space_constraint(x, pltpu.HBM)


def _dot(a, b):
    return jnp.dot(a, b, preferred_element_type=F32)


def note(myself, hot_ids, local_slot, embedding, groups):
    rows, width = embedding.shape
    hots, tiles = hot_ids.shape[0], local_slot.shape[0]

    def body(myself_ref, hot_hbm, slot_hbm, emb_hbm, out_ref, emb_ref, hot_ref, slot_ref, page, sems):
        hot_copy = pltpu.make_async_copy(hot_hbm, hot_ref, sems.at[0])
        slot_copy = pltpu.make_async_copy(slot_hbm, slot_ref, sems.at[1])
        emb_copy = pltpu.make_async_copy(emb_hbm, emb_ref, sems.at[2])
        hot_copy.start()
        slot_copy.start()
        emb_copy.start()
        page[...] = jnp.zeros((NOTE, width), F32)
        hot_copy.wait()
        within = hot_ref[...] - myself_ref[0] * rows
        row = jnp.max(jnp.where((within >= 0) & (within < rows), within, -1))
        start = pl.multiple_of((jnp.maximum(row, 0) // NOTE) * NOTE, NOTE)
        slot_copy.wait()
        page[1:2, :tiles] = slot_ref[...].astype(F32)
        emb_copy.wait()
        at = lax.broadcasted_iota(I32, (NOTE, width), 0)
        mine = jnp.where(at == row - start, emb_ref[pl.ds(start, NOTE), :].astype(F32), 0.0)
        page[0:1, :] = jnp.sum(mine, axis=0, keepdims=True)
        out_ref[...] = jnp.broadcast_to(page[...].astype(BF16)[None], (groups, NOTE, width))

    hbm = pl.BlockSpec(memory_space=pltpu.HBM)
    vmem = pl.BlockSpec(memory_space=pltpu.VMEM)
    return pl.pallas_call(
        body,
        out_shape=[pltpu.VMEM((groups, NOTE, width), BF16), pltpu.VMEM((rows, width), BF16)],
        in_specs=[pl.BlockSpec(memory_space=pltpu.SMEM), hbm, hbm, hbm],
        out_specs=[vmem, vmem],
        scratch_shapes=[
            pltpu.VMEM((1, hots), I32),
            pltpu.VMEM((1, tiles), I32),
            pltpu.VMEM((NOTE, width), F32),
            pltpu.SemaphoreType.DMA((3,)),
        ],
        compiler_params=_params(1),
        name="note",
    )(myself, _far(hot_ids.reshape(1, hots)), _far(local_slot.reshape(1, tiles)), _far(embedding))


def pick_rows(send_rows, send_count, embedding):
    rows, width = embedding.shape
    doms, cap = send_rows.shape
    half = width // 2
    step = 32
    parts = rows // 128

    def body(rows_ref, count_ref, emb_ref, out_hbm, out_ref, sems):
        slot = lax.broadcasted_iota(I32, (cap, doms), 0)
        index = jnp.where(slot < count_ref[...], rows_ref[...], -1)
        low = (index & 127).astype(F32)
        high = (index >> 7).astype(F32)
        lane = lax.broadcasted_iota(I32, (cap, 128), 1).astype(F32).astype(BF16)
        one, zero = jnp.ones((), BF16), jnp.zeros((), BF16)
        copies = []
        for i in range(0, doms, step):
            chosen = []
            for p in range(i, i + step):
                low_p = jnp.broadcast_to(low[:, p : p + 1], (cap, 128)).astype(BF16)
                high_p = jnp.broadcast_to(high[:, p : p + 1], (cap, 128)).astype(BF16)
                at = jnp.where(low_p == lane, one, zero)
                chosen.append(
                    jnp.concatenate([jnp.where(high_p == jnp.asarray(k, BF16), at, zero) for k in range(parts)], axis=1)
                )
            got = _dot(jnp.concatenate(chosen, axis=0), emb_ref[...]).astype(BF16).reshape(step, cap, width)
            out_ref[i : i + step, :cap, :] = got[:, :, :half]
            out_ref[i : i + step, cap : 2 * cap, :] = got[:, :, half:]
            copies.append(
                pltpu.make_async_copy(
                    out_ref.at[i : i + step], out_hbm.at[i : i + step, : 2 * cap, :], sems.at[i // step]
                )
            )
            copies[-1].start()
        for copy in copies:
            copy.wait()

    return pl.pallas_call(
        body,
        out_shape=pltpu.HBM((doms, 2 * cap + 8, half), BF16),
        in_specs=[
            pl.BlockSpec((cap, doms), lambda: (0, 0)),
            pl.BlockSpec((1, doms), lambda: (0, 0)),
            pl.BlockSpec((rows, width), lambda: (0, 0)),
        ],
        out_specs=pl.BlockSpec(memory_space=pl.ANY),
        scratch_shapes=[pltpu.VMEM((doms, 2 * cap, half), BF16), pltpu.SemaphoreType.DMA((doms // step,))],
        compiler_params=_params(24),
        name="pick_rows",
    )(_near(send_rows.T), _near(send_count.reshape(1, doms)), _near(embedding))


def add_drivers(notes, message):
    doms, length, half = message.shape
    groups = notes.shape[0]

    def body(notes_ref, _, out_ref, page, sem):
        at = lax.broadcasted_iota(I32, (8, half), 0)
        last = jnp.zeros((8, half), F32)
        for g in range(groups):
            row = notes_ref[g].astype(F32)[0:1, :]
            last = jnp.where(at == g, row[:, :half], last)
            last = jnp.where(at == groups + g, row[:, half:], last)
        page[...] = jnp.broadcast_to(last[None], (doms, 8, half)).astype(BF16)
        copy = pltpu.make_async_copy(page, out_ref.at[:, pl.ds(length - 8, 8), :], sem)
        copy.start()
        copy.wait()

    return pl.pallas_call(
        body,
        out_shape=jax.ShapeDtypeStruct(message.shape, BF16),
        in_specs=[pl.BlockSpec(notes.shape, lambda: (0, 0, 0)), pl.BlockSpec(memory_space=pl.ANY)],
        out_specs=pl.BlockSpec(memory_space=pl.ANY),
        scratch_shapes=[pltpu.VMEM((doms, 8, half), BF16), pltpu.SemaphoreType.DMA(())],
        input_output_aliases={1: 0},
        compiler_params=_params(2),
        name="add_drivers",
    )(notes, _far(message))


def pick_tiles(group, slots, embedding, first_weight, second_weight, tile):
    groups, tiles = slots.shape
    rows, width = embedding.shape
    each = tiles // groups
    a, b = first_weight.shape[0], second_weight.shape[0]
    length = each * tile + a + b

    def body(group_ref, slots_ref, emb_ref, first_ref, second_ref, *rest):
        outs, (listed, sems) = rest[: groups - 1], rest[groups - 1 :]
        me = group_ref[0]
        copies = []
        for k in range(1, groups):
            out = outs[k - 1]
            other = (me + k) % groups
            copies.append(pltpu.make_async_copy(first_ref, out.at[pl.ds(each * tile, a), :], sems.at[k - 1, each]))
            copies.append(
                pltpu.make_async_copy(second_ref, out.at[pl.ds(each * tile + a, b), :], sems.at[k - 1, each + 1])
            )
            for j in range(each):
                listed[k - 1, j] = 0

            def look(t, found, k=k, other=other):
                tile_at = slots_ref[other, t]
                hit = (tile_at >= me * tiles) & (tile_at < (me + 1) * tiles)

                @pl.when(hit)
                def _():
                    listed[k - 1, jnp.minimum(found, each - 1)] = tile_at - me * tiles

                return found + hit.astype(I32)

            lax.fori_loop(0, tiles, look, jnp.zeros((), I32))
            for j in range(each):
                start = pl.multiple_of(listed[k - 1, j] * tile, tile)
                copies.append(
                    pltpu.make_async_copy(
                        emb_ref.at[pl.ds(start, tile), :], out.at[pl.ds(j * tile, tile), :], sems.at[k - 1, j]
                    )
                )
        for copy in copies:
            copy.start()
        for copy in copies:
            copy.wait()

    hbm = pl.BlockSpec(memory_space=pl.ANY)
    smem = pl.BlockSpec(memory_space=pltpu.SMEM)
    return pl.pallas_call(
        body,
        out_shape=[pltpu.HBM((length, width), BF16)] * (groups - 1),
        in_specs=[smem, smem, hbm, hbm, hbm],
        out_specs=[hbm] * (groups - 1),
        scratch_shapes=[
            pltpu.SMEM((groups - 1, each), I32),
            pltpu.SemaphoreType.DMA((groups - 1, each + 2)),
        ],
        compiler_params=_params(2),
        name="pick_tiles",
    )(group, slots, _near(embedding), first_weight, second_weight)


def ready(group, slot, embedding, arrived, first_weight, second_weight, tile):
    width = embedding.shape[1]
    tiles = slot.shape[0]
    groups = len(arrived) + 1
    each = tiles // groups
    a, b = first_weight.shape[0], second_weight.shape[0]

    def body(group_ref, slot_ref, emb_ref, own_a, own_b, *rest):
        parts = rest[: groups - 1]
        tiles_hbm, first_hbm, second_hbm, tiles_ref, first_ref, second_ref, tile_sems, sems, out_sems = rest[groups - 1 :]
        me = group_ref[0]
        firsts, seconds = [], []
        for k in range(groups):
            other = (me + groups - k) % groups
            from_a = own_a if k == 0 else parts[k - 1].at[pl.ds(each * tile, a), :]
            from_b = own_b if k == 0 else parts[k - 1].at[pl.ds(each * tile + a, b), :]
            to_a = first_ref.at[pl.ds(pl.multiple_of(other * a, a), a), :]
            to_b = second_ref.at[pl.ds(pl.multiple_of(other * b, b), b), :]
            firsts.append(pltpu.make_async_copy(from_a, to_a, sems.at[0, k]))
            seconds.append(pltpu.make_async_copy(from_b, to_b, sems.at[1, k]))

        def send(t, counts):
            tile_at = slot_ref[t]
            source = sum((tile_at >= tiles * g).astype(I32) for g in range(1, groups))
            spot = sum(jnp.where(source == g, counts[g], 0) for g in range(groups))
            away = (me + groups - source) % groups
            for k in range(groups):

                @pl.when(away == k)
                def _(k=k):
                    if k == 0:
                        at = pl.multiple_of((tile_at - source * tiles) * tile, tile)
                        here = emb_ref.at[pl.ds(at, tile), :]
                    else:
                        at = pl.multiple_of(jnp.minimum(spot, each - 1) * tile, tile)
                        here = parts[k - 1].at[pl.ds(at, tile), :]
                    pltpu.make_async_copy(here, tiles_ref.at[t], tile_sems.at[t]).start()

            return tuple(counts[g] + (source == g).astype(I32) for g in range(groups))

        lax.fori_loop(0, tiles, send, (jnp.zeros((), I32),) * groups)
        for copy in (*firsts, *seconds):
            copy.start()
        for t in range(tiles):
            pltpu.make_async_copy(emb_ref.at[pl.ds(0, tile), :], tiles_ref.at[t], tile_sems.at[t]).wait()
        leaving = [pltpu.make_async_copy(tiles_ref, tiles_hbm, out_sems.at[0])]
        leaving[-1].start()
        for n, (copies, here, there) in enumerate(
            ((firsts, first_ref, first_hbm), (seconds, second_ref, second_hbm)), start=1
        ):
            for copy in copies:
                copy.wait()
            leaving.append(pltpu.make_async_copy(here, there, out_sems.at[n]))
            leaving[-1].start()
        for copy in leaving:
            copy.wait()

    smem = pl.BlockSpec(memory_space=pltpu.SMEM)
    hbm = pl.BlockSpec(memory_space=pltpu.HBM)
    return pl.pallas_call(
        body,
        out_shape=[
            pltpu.HBM((tiles, tile, width), BF16),
            pltpu.HBM((groups * a, width), BF16),
            pltpu.HBM((groups * b, width), BF16),
        ],
        in_specs=[smem, smem, pl.BlockSpec(memory_space=pltpu.VMEM)] + [hbm] * (2 + len(arrived)),
        out_specs=[hbm] * 3,
        scratch_shapes=[
            pltpu.VMEM((tiles, tile, width), BF16),
            pltpu.VMEM((groups * a, width), BF16),
            pltpu.VMEM((groups * b, width), BF16),
            pltpu.SemaphoreType.DMA((tiles,)),
            pltpu.SemaphoreType.DMA((2, groups)),
            pltpu.SemaphoreType.DMA((3,)),
        ],
        compiler_params=_params(4),
        name="ready",
    )(group, slot, _near(embedding), *map(_far, (first_weight, second_weight, *arrived)))


def after_halo(
    halo_slot, halo, driver_at, local_tiles, adjacency, driver_weight, embedding, first, second, feats, feature_weight,
    first_bias, second_bias,
):
    rows, width = embedding.shape
    tiles, _, tile, _ = adjacency.shape
    doms, length, half = halo.shape
    cap = (length - 8) // 2
    hots = driver_weight.shape[1]
    many = tiles // 2
    block = many * tile
    per = tile // cap

    def body(local_hbm, adj_hbm, *rest):
        small_hbm, rest = rest[:7], rest[7:]
        halo_ref, at_ref, dw_ref, emb_ref, out_hbm, local_ref, adj_ref, *rest = rest
        small, (out, sems, in_sems, out_sems) = rest[:7], rest[7:]
        slot_ref, first_ref, feat_ref, fw_ref, first_bias_ref, second_ref, second_bias_ref = small
        blocks = tiles // many
        smalls = [pltpu.make_async_copy(x, y, sems.at[n]) for n, (x, y) in enumerate(zip(small_hbm, small))]
        smalls[0].start()
        arriving = []
        for n in range(blocks):
            these = pl.ds(n * many, many)
            arriving.append(
                (
                    pltpu.make_async_copy(local_hbm.at[these], local_ref.at[these], in_sems.at[0, n]),
                    pltpu.make_async_copy(adj_hbm.at[these], adj_ref.at[these], in_sems.at[1, n]),
                )
            )
            for copy in arriving[-1]:
                copy.start()
            if n == 0:
                for copy in smalls[1:]:
                    copy.start()
        column = lax.broadcasted_iota(I32, (hots, doms * 8), 1)
        ends = halo_ref[:, 2 * cap :, :].reshape(doms * 8, half)
        left = jnp.where(column == at_ref[...], 1.0, 0.0).astype(BF16)
        right = jnp.where(column == at_ref[...] + 4, 1.0, 0.0).astype(BF16)
        drivers = jnp.concatenate([_dot(left, ends).astype(BF16), _dot(right, ends).astype(BF16)], axis=1)
        smalls[0].wait()
        copies = []
        for n in range(blocks):
            for copy in arriving[n]:
                copy.wait()
            aggregate = []
            for t in range(n * many, (n + 1) * many):
                which = pl.ds(pl.multiple_of(slot_ref[0, t] * per, per), per)
                halo_tile = jnp.concatenate(
                    [
                        halo_ref[which, :cap, :].reshape(tile, half),
                        halo_ref[which, cap : 2 * cap, :].reshape(tile, half),
                    ],
                    axis=1,
                )
                edges = jnp.concatenate([adj_ref[t, 0], adj_ref[t, 1], dw_ref[t * tile : (t + 1) * tile, :]], axis=1)
                sources = jnp.concatenate([local_ref[t], halo_tile, drivers], axis=0)
                aggregate.append(_dot(edges, sources).astype(BF16))
            if n == 0:
                for copy in smalls[1:]:
                    copy.wait()
            here = slice(n * block, (n + 1) * block)
            own = emb_ref[here, :]
            inner = (
                _dot(jnp.concatenate([own, jnp.concatenate(aggregate, axis=0)], axis=1), first_ref[...])
                + lax.dot_general(
                    feat_ref[:, here], fw_ref[...], (((0,), (0,)), ((), ())), preferred_element_type=F32
                )
                + first_bias_ref[...]
            )
            activated = (0.5 * inner * (1.0 + lax.erf(inner * (0.5**0.5)))).astype(BF16)
            out[here, :] = (own.astype(F32) + second_bias_ref[...] + _dot(activated, second_ref[...])).astype(BF16)
            copies.append(pltpu.make_async_copy(out.at[here, :], out_hbm.at[here, :], out_sems.at[n]))
            copies[-1].start()
        for copy in copies:
            copy.wait()

    hbm = pl.BlockSpec(memory_space=pltpu.HBM)
    vmem = pl.BlockSpec(memory_space=pltpu.VMEM)
    smalls = (halo_slot.reshape(1, tiles), first, feats, feature_weight, first_bias, second, second_bias)
    return pl.pallas_call(
        body,
        out_shape=jax.ShapeDtypeStruct((rows, width), BF16),
        in_specs=[hbm] * 9 + [vmem] * 4,
        out_specs=hbm,
        scratch_shapes=[
            pltpu.VMEM(local_tiles.shape, BF16),
            pltpu.VMEM(adjacency.shape, BF16),
            pltpu.SMEM((1, tiles), I32),
            *[pltpu.VMEM(x.shape, x.dtype) for x in smalls[1:]],
            pltpu.VMEM((rows, width), BF16),
            pltpu.SemaphoreType.DMA((7,)),
            pltpu.SemaphoreType.DMA((2, tiles // many)),
            pltpu.SemaphoreType.DMA((tiles // many,)),
        ],
        compiler_params=_params(24),
        name="after_halo",
    )(
        *map(_far, (local_tiles, adjacency, *smalls)),
        *map(_near, (halo, driver_at, driver_weight, embedding)),
    )


def per_device(
    embedding,
    scenario_feats,
    adjacency,
    driver_weight,
    local_slot,
    halo_slot,
    send_rows,
    send_count,
    hot_ids,
    first_weight,
    feature_weight,
    first_bias,
    second_weight,
    second_bias,
):
    rows, width = embedding.shape
    tile = adjacency.shape[-1]
    tiles = rows // tile
    groups = lax.axis_size("scen")
    myself = lax.axis_index(("dom", "scen")).astype(I32).reshape(1)
    group = lax.axis_index("scen").astype(I32).reshape(1)

    page, embedding = note(myself, hot_ids, local_slot, embedding, groups)
    notes = lax.all_to_all(page, "scen", split_axis=0, concat_axis=0, tiled=True)
    message = pick_rows(send_rows, send_count, embedding)
    message = add_drivers(notes, message)
    halo = lax.all_to_all(message, "dom", split_axis=0, concat_axis=0, tiled=True)

    slots = notes[:, 1, :tiles].astype(I32)
    leaving = pick_tiles(group, slots, embedding, first_weight, second_weight, tile)
    arrived = [
        lax.ppermute(x, "scen", [(g, (g + k) % groups) for g in range(groups)])
        for k, x in enumerate(leaving, start=1)
    ]
    local_tiles, first, second = ready(group, local_slot, embedding, arrived, first_weight, second_weight, tile)
    owner = hot_ids // rows
    driver_at = (owner // groups * 8 + owner % groups).reshape(-1, 1)
    return after_halo(
        halo_slot,
        halo,
        driver_at,
        local_tiles,
        adjacency,
        driver_weight,
        embedding,
        first,
        second,
        scenario_feats,
        feature_weight,
        first_bias.reshape(1, width),
        second_bias.reshape(1, width),
    )


def solution(mesh):
    return jax.shard_map(
        per_device,
        mesh=mesh,
        in_specs=(
            P(("dom", "scen"), None),
            P(None, ("dom", "scen")),
            P(("dom", "scen"), None, None, None),
            P(("dom", "scen"), None),
            P(("dom", "scen")),
            P(("dom", "scen")),
            P(("dom", "scen"), None),
            P(("dom", "scen")),
            P(),
            P("scen", None),
            P(),
            P(),
            P("scen", None),
            P(),
        ),
        out_specs=P(("dom", "scen"), None),
        check_vma=False,
    )
```

```python
import jax
import jax.numpy as jnp
from jax import lax
from jax.experimental import pallas as pl
from jax.experimental.pallas import tpu as pltpu
from jax.sharding import PartitionSpec as P

BF16, F32, I32 = jnp.bfloat16, jnp.float32, jnp.int32
NOTE = 16


def _params(mebibytes):
    return pltpu.CompilerParams(vmem_limit_bytes=mebibytes * 1024 * 1024)


def _near(x):
    return pltpu.with_memory_space_constraint(x, pltpu.VMEM)


def _far(x):
    return pltpu.with_memory_space_constraint(x, pltpu.HBM)


def _dot(a, b):
    return jnp.dot(a, b, preferred_element_type=F32)


def note(myself, hot_ids, local_slot, embedding, groups):
    rows, width = embedding.shape
    hots, tiles = hot_ids.shape[0], local_slot.shape[0]

    def body(myself_ref, hot_hbm, slot_hbm, emb_hbm, out_ref, emb_ref, hot_ref, slot_ref, page, sems):
        hot_copy = pltpu.make_async_copy(hot_hbm, hot_ref, sems.at[0])
        slot_copy = pltpu.make_async_copy(slot_hbm, slot_ref, sems.at[1])
        emb_copy = pltpu.make_async_copy(emb_hbm, emb_ref, sems.at[2])
        hot_copy.start()
        slot_copy.start()
        emb_copy.start()
        page[...] = jnp.zeros((NOTE, width), F32)
        hot_copy.wait()
        within = hot_ref[...] - myself_ref[0] * rows
        row = jnp.max(jnp.where((within >= 0) & (within < rows), within, -1))
        start = pl.multiple_of((jnp.maximum(row, 0) // NOTE) * NOTE, NOTE)
        slot_copy.wait()
        page[1:2, :tiles] = slot_ref[...].astype(F32)
        emb_copy.wait()
        at = lax.broadcasted_iota(I32, (NOTE, width), 0)
        mine = jnp.where(at == row - start, emb_ref[pl.ds(start, NOTE), :].astype(F32), 0.0)
        page[0:1, :] = jnp.sum(mine, axis=0, keepdims=True)
        out_ref[...] = jnp.broadcast_to(page[...].astype(BF16)[None], (groups, NOTE, width))

    hbm = pl.BlockSpec(memory_space=pltpu.HBM)
    vmem = pl.BlockSpec(memory_space=pltpu.VMEM)
    return pl.pallas_call(
        body,
        out_shape=[pltpu.VMEM((groups, NOTE, width), BF16), pltpu.VMEM((rows, width), BF16)],
        in_specs=[pl.BlockSpec(memory_space=pltpu.SMEM), hbm, hbm, hbm],
        out_specs=[vmem, vmem],
        scratch_shapes=[
            pltpu.VMEM((1, hots), I32),
            pltpu.VMEM((1, tiles), I32),
            pltpu.VMEM((NOTE, width), F32),
            pltpu.SemaphoreType.DMA((3,)),
        ],
        compiler_params=_params(1),
        name="note",
    )(myself, _far(hot_ids.reshape(1, hots)), _far(local_slot.reshape(1, tiles)), _far(embedding))


def pick_rows(send_rows, send_count, embedding):
    rows, width = embedding.shape
    doms, cap = send_rows.shape
    half = width // 2
    step = 32
    parts = rows // 128

    def body(rows_ref, count_ref, emb_ref, out_hbm, out_ref, sems):
        slot = lax.broadcasted_iota(I32, (cap, doms), 0)
        index = jnp.where(slot < count_ref[...], rows_ref[...], -1)
        low = (index & 127).astype(F32)
        high = (index >> 7).astype(F32)
        lane = lax.broadcasted_iota(I32, (cap, 128), 1).astype(F32).astype(BF16)
        one, zero = jnp.ones((), BF16), jnp.zeros((), BF16)
        copies = []
        for i in range(0, doms, step):
            chosen = []
            for p in range(i, i + step):
                low_p = jnp.broadcast_to(low[:, p : p + 1], (cap, 128)).astype(BF16)
                high_p = jnp.broadcast_to(high[:, p : p + 1], (cap, 128)).astype(BF16)
                at = jnp.where(low_p == lane, one, zero)
                chosen.append(
                    jnp.concatenate([jnp.where(high_p == jnp.asarray(k, BF16), at, zero) for k in range(parts)], axis=1)
                )
            got = _dot(jnp.concatenate(chosen, axis=0), emb_ref[...]).astype(BF16).reshape(step, cap, width)
            out_ref[i : i + step, :cap, :] = got[:, :, :half]
            out_ref[i : i + step, cap : 2 * cap, :] = got[:, :, half:]
            copies.append(
                pltpu.make_async_copy(
                    out_ref.at[i : i + step], out_hbm.at[i : i + step, : 2 * cap, :], sems.at[i // step]
                )
            )
            copies[-1].start()
        for copy in copies:
            copy.wait()

    return pl.pallas_call(
        body,
        out_shape=pltpu.HBM((doms, 2 * cap + 8, half), BF16),
        in_specs=[
            pl.BlockSpec((cap, doms), lambda: (0, 0)),
            pl.BlockSpec((1, doms), lambda: (0, 0)),
            pl.BlockSpec((rows, width), lambda: (0, 0)),
        ],
        out_specs=pl.BlockSpec(memory_space=pl.ANY),
        scratch_shapes=[pltpu.VMEM((doms, 2 * cap, half), BF16), pltpu.SemaphoreType.DMA((doms // step,))],
        compiler_params=_params(24),
        name="pick_rows",
    )(_near(send_rows.T), _near(send_count.reshape(1, doms)), _near(embedding))


def add_drivers(notes, message):
    doms, length, half = message.shape
    groups = notes.shape[0]

    def body(notes_ref, _, out_ref, page, sem):
        at = lax.broadcasted_iota(I32, (8, half), 0)
        last = jnp.zeros((8, half), F32)
        for g in range(groups):
            row = notes_ref[g].astype(F32)[0:1, :]
            last = jnp.where(at == g, row[:, :half], last)
            last = jnp.where(at == groups + g, row[:, half:], last)
        page[...] = jnp.broadcast_to(last[None], (doms, 8, half)).astype(BF16)
        copy = pltpu.make_async_copy(page, out_ref.at[:, pl.ds(length - 8, 8), :], sem)
        copy.start()
        copy.wait()

    return pl.pallas_call(
        body,
        out_shape=jax.ShapeDtypeStruct(message.shape, BF16),
        in_specs=[pl.BlockSpec(notes.shape, lambda: (0, 0, 0)), pl.BlockSpec(memory_space=pl.ANY)],
        out_specs=pl.BlockSpec(memory_space=pl.ANY),
        scratch_shapes=[pltpu.VMEM((doms, 8, half), BF16), pltpu.SemaphoreType.DMA(())],
        input_output_aliases={1: 0},
        compiler_params=_params(2),
        name="add_drivers",
    )(notes, _far(message))


def pick_tiles(group, slots, embedding, first_weight, second_weight, tile):
    groups, tiles = slots.shape
    rows, width = embedding.shape
    each = tiles // groups
    a, b = first_weight.shape[0], second_weight.shape[0]
    length = each * tile + a + b

    def body(group_ref, slots_ref, emb_ref, first_ref, second_ref, *rest):
        outs, (listed, sems) = rest[: groups - 1], rest[groups - 1 :]
        me = group_ref[0]
        copies = []
        for k in range(1, groups):
            out = outs[k - 1]
            other = (me + k) % groups
            copies.append(pltpu.make_async_copy(first_ref, out.at[pl.ds(each * tile, a), :], sems.at[k - 1, each]))
            copies.append(
                pltpu.make_async_copy(second_ref, out.at[pl.ds(each * tile + a, b), :], sems.at[k - 1, each + 1])
            )
            for j in range(each):
                listed[k - 1, j] = 0

            def look(t, found, k=k, other=other):
                tile_at = slots_ref[other, t]
                hit = (tile_at >= me * tiles) & (tile_at < (me + 1) * tiles)

                @pl.when(hit)
                def _():
                    listed[k - 1, jnp.minimum(found, each - 1)] = tile_at - me * tiles

                return found + hit.astype(I32)

            lax.fori_loop(0, tiles, look, jnp.zeros((), I32))
            for j in range(each):
                start = pl.multiple_of(listed[k - 1, j] * tile, tile)
                copies.append(
                    pltpu.make_async_copy(
                        emb_ref.at[pl.ds(start, tile), :], out.at[pl.ds(j * tile, tile), :], sems.at[k - 1, j]
                    )
                )
        for copy in copies:
            copy.start()
        for copy in copies:
            copy.wait()

    hbm = pl.BlockSpec(memory_space=pl.ANY)
    smem = pl.BlockSpec(memory_space=pltpu.SMEM)
    return pl.pallas_call(
        body,
        out_shape=[pltpu.HBM((length, width), BF16)] * (groups - 1),
        in_specs=[smem, smem, hbm, hbm, hbm],
        out_specs=[hbm] * (groups - 1),
        scratch_shapes=[
            pltpu.SMEM((groups - 1, each), I32),
            pltpu.SemaphoreType.DMA((groups - 1, each + 2)),
        ],
        compiler_params=_params(2),
        name="pick_tiles",
    )(group, slots, _near(embedding), first_weight, second_weight)


def ready(group, slot, embedding, arrived, first_weight, second_weight, tile):
    width = embedding.shape[1]
    tiles = slot.shape[0]
    groups = len(arrived) + 1
    each = tiles // groups
    a, b = first_weight.shape[0], second_weight.shape[0]

    def body(group_ref, slot_ref, emb_ref, own_a, own_b, *rest):
        parts = rest[: groups - 1]
        tiles_hbm, first_hbm, second_hbm, tiles_ref, first_ref, second_ref, tile_sems, sems, out_sems = rest[groups - 1 :]
        me = group_ref[0]
        firsts, seconds = [], []
        for k in range(groups):
            other = (me + groups - k) % groups
            from_a = own_a if k == 0 else parts[k - 1].at[pl.ds(each * tile, a), :]
            from_b = own_b if k == 0 else parts[k - 1].at[pl.ds(each * tile + a, b), :]
            to_a = first_ref.at[pl.ds(pl.multiple_of(other * a, a), a), :]
            to_b = second_ref.at[pl.ds(pl.multiple_of(other * b, b), b), :]
            firsts.append(pltpu.make_async_copy(from_a, to_a, sems.at[0, k]))
            seconds.append(pltpu.make_async_copy(from_b, to_b, sems.at[1, k]))

        def send(t, counts):
            tile_at = slot_ref[t]
            source = sum((tile_at >= tiles * g).astype(I32) for g in range(1, groups))
            spot = sum(jnp.where(source == g, counts[g], 0) for g in range(groups))
            away = (me + groups - source) % groups
            for k in range(groups):

                @pl.when(away == k)
                def _(k=k):
                    if k == 0:
                        at = pl.multiple_of((tile_at - source * tiles) * tile, tile)
                        here = emb_ref.at[pl.ds(at, tile), :]
                    else:
                        at = pl.multiple_of(jnp.minimum(spot, each - 1) * tile, tile)
                        here = parts[k - 1].at[pl.ds(at, tile), :]
                    pltpu.make_async_copy(here, tiles_ref.at[t], tile_sems.at[t]).start()

            return tuple(counts[g] + (source == g).astype(I32) for g in range(groups))

        lax.fori_loop(0, tiles, send, (jnp.zeros((), I32),) * groups)
        for copy in (*firsts, *seconds):
            copy.start()
        for t in range(tiles):
            pltpu.make_async_copy(emb_ref.at[pl.ds(0, tile), :], tiles_ref.at[t], tile_sems.at[t]).wait()
        leaving = [pltpu.make_async_copy(tiles_ref, tiles_hbm, out_sems.at[0])]
        leaving[-1].start()
        for n, (copies, here, there) in enumerate(
            ((firsts, first_ref, first_hbm), (seconds, second_ref, second_hbm)), start=1
        ):
            for copy in copies:
                copy.wait()
            leaving.append(pltpu.make_async_copy(here, there, out_sems.at[n]))
            leaving[-1].start()
        for copy in leaving:
            copy.wait()

    smem = pl.BlockSpec(memory_space=pltpu.SMEM)
    hbm = pl.BlockSpec(memory_space=pltpu.HBM)
    return pl.pallas_call(
        body,
        out_shape=[
            pltpu.HBM((tiles, tile, width), BF16),
            pltpu.HBM((groups * a, width), BF16),
            pltpu.HBM((groups * b, width), BF16),
        ],
        in_specs=[smem, smem, pl.BlockSpec(memory_space=pltpu.VMEM)] + [hbm] * (2 + len(arrived)),
        out_specs=[hbm] * 3,
        scratch_shapes=[
            pltpu.VMEM((tiles, tile, width), BF16),
            pltpu.VMEM((groups * a, width), BF16),
            pltpu.VMEM((groups * b, width), BF16),
            pltpu.SemaphoreType.DMA((tiles,)),
            pltpu.SemaphoreType.DMA((2, groups)),
            pltpu.SemaphoreType.DMA((3,)),
        ],
        compiler_params=_params(4),
        name="ready",
    )(group, slot, _near(embedding), *map(_far, (first_weight, second_weight, *arrived)))


def after_halo(
    halo_slot, halo, driver_at, local_tiles, adjacency, driver_weight, embedding, first, second, feats, feature_weight,
    first_bias, second_bias,
):
    rows, width = embedding.shape
    tiles, _, tile, _ = adjacency.shape
    doms, length, half = halo.shape
    cap = (length - 8) // 2
    hots = driver_weight.shape[1]
    many = tiles // 2
    block = many * tile
    per = tile // cap

    def body(local_hbm, adj_hbm, *rest):
        small_hbm, rest = rest[:7], rest[7:]
        halo_ref, at_ref, dw_ref, emb_ref, out_hbm, local_ref, adj_ref, *rest = rest
        small, (out, sems, in_sems, out_sems) = rest[:7], rest[7:]
        slot_ref, first_ref, feat_ref, fw_ref, first_bias_ref, second_ref, second_bias_ref = small
        blocks = tiles // many
        smalls = [pltpu.make_async_copy(x, y, sems.at[n]) for n, (x, y) in enumerate(zip(small_hbm, small))]
        smalls[0].start()
        arriving = []
        for n in range(blocks):
            these = pl.ds(n * many, many)
            arriving.append(
                (
                    pltpu.make_async_copy(local_hbm.at[these], local_ref.at[these], in_sems.at[0, n]),
                    pltpu.make_async_copy(adj_hbm.at[these], adj_ref.at[these], in_sems.at[1, n]),
                )
            )
            for copy in arriving[-1]:
                copy.start()
            if n == 0:
                for copy in smalls[1:]:
                    copy.start()
        column = lax.broadcasted_iota(I32, (hots, doms * 8), 1)
        ends = halo_ref[:, 2 * cap :, :].reshape(doms * 8, half)
        left = jnp.where(column == at_ref[...], 1.0, 0.0).astype(BF16)
        right = jnp.where(column == at_ref[...] + 4, 1.0, 0.0).astype(BF16)
        drivers = jnp.concatenate([_dot(left, ends).astype(BF16), _dot(right, ends).astype(BF16)], axis=1)
        smalls[0].wait()
        copies = []
        for n in range(blocks):
            if n == 0:
                for copy in arriving[0]:
                    copy.wait()
            aggregate = []
            for t in range(n * many, (n + 1) * many):
                which = pl.ds(pl.multiple_of(slot_ref[0, t] * per, per), per)
                halo_tile = jnp.concatenate(
                    [
                        halo_ref[which, :cap, :].reshape(tile, half),
                        halo_ref[which, cap : 2 * cap, :].reshape(tile, half),
                    ],
                    axis=1,
                )
                edges = jnp.concatenate([adj_ref[t, 0], adj_ref[t, 1], dw_ref[t * tile : (t + 1) * tile, :]], axis=1)
                sources = jnp.concatenate([local_ref[t], halo_tile, drivers], axis=0)
                aggregate.append(_dot(edges, sources).astype(BF16))
            if n == 0:
                for copy in (*smalls[1:], *arriving[1]):
                    copy.wait()
            here = slice(n * block, (n + 1) * block)
            own = emb_ref[here, :]
            inner = (
                _dot(jnp.concatenate([own, jnp.concatenate(aggregate, axis=0)], axis=1), first_ref[...])
                + lax.dot_general(
                    feat_ref[:, here], fw_ref[...], (((0,), (0,)), ((), ())), preferred_element_type=F32
                )
                + first_bias_ref[...]
            )
            activated = (0.5 * inner * (1.0 + lax.erf(inner * (0.5**0.5)))).astype(BF16)
            out[here, :] = (own.astype(F32) + second_bias_ref[...] + _dot(activated, second_ref[...])).astype(BF16)
            copies.append(pltpu.make_async_copy(out.at[here, :], out_hbm.at[here, :], out_sems.at[n]))
            copies[-1].start()
        for copy in copies:
            copy.wait()

    hbm = pl.BlockSpec(memory_space=pltpu.HBM)
    vmem = pl.BlockSpec(memory_space=pltpu.VMEM)
    smalls = (halo_slot.reshape(1, tiles), first, feats, feature_weight, first_bias, second, second_bias)
    return pl.pallas_call(
        body,
        out_shape=jax.ShapeDtypeStruct((rows, width), BF16),
        in_specs=[hbm] * 9 + [vmem] * 4,
        out_specs=hbm,
        scratch_shapes=[
            pltpu.VMEM(local_tiles.shape, BF16),
            pltpu.VMEM(adjacency.shape, BF16),
            pltpu.SMEM((1, tiles), I32),
            *[pltpu.VMEM(x.shape, x.dtype) for x in smalls[1:]],
            pltpu.VMEM((rows, width), BF16),
            pltpu.SemaphoreType.DMA((7,)),
            pltpu.SemaphoreType.DMA((2, tiles // many)),
            pltpu.SemaphoreType.DMA((tiles // many,)),
        ],
        compiler_params=_params(24),
        name="after_halo",
    )(
        *map(_far, (local_tiles, adjacency, *smalls)),
        *map(_near, (halo, driver_at, driver_weight, embedding)),
    )


def per_device(
    embedding,
    scenario_feats,
    adjacency,
    driver_weight,
    local_slot,
    halo_slot,
    send_rows,
    send_count,
    hot_ids,
    first_weight,
    feature_weight,
    first_bias,
    second_weight,
    second_bias,
):
    rows, width = embedding.shape
    tile = adjacency.shape[-1]
    tiles = rows // tile
    groups = lax.axis_size("scen")
    myself = lax.axis_index(("dom", "scen")).astype(I32).reshape(1)
    group = lax.axis_index("scen").astype(I32).reshape(1)

    page, embedding = note(myself, hot_ids, local_slot, embedding, groups)
    notes = lax.all_to_all(page, "scen", split_axis=0, concat_axis=0, tiled=True)
    message = pick_rows(send_rows, send_count, embedding)
    message = add_drivers(notes, message)
    halo = lax.all_to_all(message, "dom", split_axis=0, concat_axis=0, tiled=True)

    slots = notes[:, 1, :tiles].astype(I32)
    leaving = pick_tiles(group, slots, embedding, first_weight, second_weight, tile)
    arrived = [
        lax.ppermute(x, "scen", [(g, (g + k) % groups) for g in range(groups)])
        for k, x in enumerate(leaving, start=1)
    ]
    local_tiles, first, second = ready(group, local_slot, embedding, arrived, first_weight, second_weight, tile)
    owner = hot_ids // rows
    driver_at = (owner // groups * 8 + owner % groups).reshape(-1, 1)
    return after_halo(
        halo_slot,
        halo,
        driver_at,
        local_tiles,
        adjacency,
        driver_weight,
        embedding,
        first,
        second,
        scenario_feats,
        feature_weight,
        first_bias.reshape(1, width),
        second_bias.reshape(1, width),
    )


def solution(mesh):
    return jax.shard_map(
        per_device,
        mesh=mesh,
        in_specs=(
            P(("dom", "scen"), None),
            P(None, ("dom", "scen")),
            P(("dom", "scen"), None, None, None),
            P(("dom", "scen"), None),
            P(("dom", "scen")),
            P(("dom", "scen")),
            P(("dom", "scen"), None),
            P(("dom", "scen")),
            P(),
            P("scen", None),
            P(),
            P(),
            P("scen", None),
            P(),
        ),
        out_specs=P(("dom", "scen"), None),
        check_vma=False,
    )
```

```python
import jax
import jax.numpy as jnp
from jax import lax
from jax.experimental import pallas as pl
from jax.experimental.pallas import tpu as pltpu
from jax.sharding import PartitionSpec as P

BF16, F32, I32 = jnp.bfloat16, jnp.float32, jnp.int32
NOTE = 16


def _params(mebibytes):
    return pltpu.CompilerParams(vmem_limit_bytes=mebibytes * 1024 * 1024)


def _near(x):
    return pltpu.with_memory_space_constraint(x, pltpu.VMEM)


def _far(x):
    return pltpu.with_memory_space_constraint(x, pltpu.HBM)


def _dot(a, b):
    return jnp.dot(a, b, preferred_element_type=F32)


def note(myself, hot_ids, local_slot, embedding, groups):
    rows, width = embedding.shape
    hots, tiles = hot_ids.shape[0], local_slot.shape[0]

    def body(myself_ref, hot_hbm, slot_hbm, emb_hbm, out_ref, emb_ref, hot_ref, slot_ref, page, sems):
        hot_copy = pltpu.make_async_copy(hot_hbm, hot_ref, sems.at[0])
        slot_copy = pltpu.make_async_copy(slot_hbm, slot_ref, sems.at[1])
        emb_copy = pltpu.make_async_copy(emb_hbm, emb_ref, sems.at[2])
        hot_copy.start()
        slot_copy.start()
        emb_copy.start()
        page[...] = jnp.zeros((NOTE, width), F32)
        hot_copy.wait()
        within = hot_ref[...] - myself_ref[0] * rows
        row = jnp.max(jnp.where((within >= 0) & (within < rows), within, -1))
        start = pl.multiple_of((jnp.maximum(row, 0) // NOTE) * NOTE, NOTE)
        slot_copy.wait()
        page[1:2, :tiles] = slot_ref[...].astype(F32)
        emb_copy.wait()
        at = lax.broadcasted_iota(I32, (NOTE, width), 0)
        mine = jnp.where(at == row - start, emb_ref[pl.ds(start, NOTE), :].astype(F32), 0.0)
        page[0:1, :] = jnp.sum(mine, axis=0, keepdims=True)
        out_ref[...] = jnp.broadcast_to(page[...].astype(BF16)[None], (groups, NOTE, width))

    hbm = pl.BlockSpec(memory_space=pltpu.HBM)
    vmem = pl.BlockSpec(memory_space=pltpu.VMEM)
    return pl.pallas_call(
        body,
        out_shape=[pltpu.VMEM((groups, NOTE, width), BF16), pltpu.VMEM((rows, width), BF16)],
        in_specs=[pl.BlockSpec(memory_space=pltpu.SMEM), hbm, hbm, hbm],
        out_specs=[vmem, vmem],
        scratch_shapes=[
            pltpu.VMEM((1, hots), I32),
            pltpu.VMEM((1, tiles), I32),
            pltpu.VMEM((NOTE, width), F32),
            pltpu.SemaphoreType.DMA((3,)),
        ],
        compiler_params=_params(1),
        name="note",
    )(myself, _far(hot_ids.reshape(1, hots)), _far(local_slot.reshape(1, tiles)), _far(embedding))


def pick_rows(send_rows, send_count, embedding):
    rows, width = embedding.shape
    doms, cap = send_rows.shape
    half = width // 2
    step = 32
    parts = rows // 128

    def body(rows_ref, count_ref, emb_ref, out_hbm, out_ref, sems):
        slot = lax.broadcasted_iota(I32, (cap, doms), 0)
        index = jnp.where(slot < count_ref[...], rows_ref[...], -1)
        low = (index & 127).astype(F32)
        high = (index >> 7).astype(F32)
        lane = lax.broadcasted_iota(I32, (cap, 128), 1).astype(F32).astype(BF16)
        one, zero = jnp.ones((), BF16), jnp.zeros((), BF16)
        copies = []
        for i in range(0, doms, step):
            chosen = []
            for p in range(i, i + step):
                low_p = jnp.broadcast_to(low[:, p : p + 1], (cap, 128)).astype(BF16)
                high_p = jnp.broadcast_to(high[:, p : p + 1], (cap, 128)).astype(BF16)
                at = jnp.where(low_p == lane, one, zero)
                chosen.append(
                    jnp.concatenate([jnp.where(high_p == jnp.asarray(k, BF16), at, zero) for k in range(parts)], axis=1)
                )
            got = _dot(jnp.concatenate(chosen, axis=0), emb_ref[...]).astype(BF16).reshape(step, cap, width)
            out_ref[i : i + step, :cap, :] = got[:, :, :half]
            out_ref[i : i + step, cap : 2 * cap, :] = got[:, :, half:]
            copies.append(
                pltpu.make_async_copy(
                    out_ref.at[i : i + step], out_hbm.at[i : i + step, : 2 * cap, :], sems.at[i // step]
                )
            )
            copies[-1].start()
        for copy in copies:
            copy.wait()

    return pl.pallas_call(
        body,
        out_shape=pltpu.HBM((doms, 2 * cap + 8, half), BF16),
        in_specs=[
            pl.BlockSpec((cap, doms), lambda: (0, 0)),
            pl.BlockSpec((1, doms), lambda: (0, 0)),
            pl.BlockSpec((rows, width), lambda: (0, 0)),
        ],
        out_specs=pl.BlockSpec(memory_space=pl.ANY),
        scratch_shapes=[pltpu.VMEM((doms, 2 * cap, half), BF16), pltpu.SemaphoreType.DMA((doms // step,))],
        compiler_params=_params(24),
        name="pick_rows",
    )(_near(send_rows.T), _near(send_count.reshape(1, doms)), _near(embedding))


def add_drivers(notes, message):
    doms, length, half = message.shape
    groups = notes.shape[0]

    def body(notes_ref, _, out_ref, page, sem):
        at = lax.broadcasted_iota(I32, (8, half), 0)
        last = jnp.zeros((8, half), F32)
        for g in range(groups):
            row = notes_ref[g].astype(F32)[0:1, :]
            last = jnp.where(at == g, row[:, :half], last)
            last = jnp.where(at == groups + g, row[:, half:], last)
        page[...] = jnp.broadcast_to(last[None], (doms, 8, half)).astype(BF16)
        copy = pltpu.make_async_copy(page, out_ref.at[:, pl.ds(length - 8, 8), :], sem)
        copy.start()
        copy.wait()

    return pl.pallas_call(
        body,
        out_shape=jax.ShapeDtypeStruct(message.shape, BF16),
        in_specs=[pl.BlockSpec(notes.shape, lambda: (0, 0, 0)), pl.BlockSpec(memory_space=pl.ANY)],
        out_specs=pl.BlockSpec(memory_space=pl.ANY),
        scratch_shapes=[pltpu.VMEM((doms, 8, half), BF16), pltpu.SemaphoreType.DMA(())],
        input_output_aliases={1: 0},
        compiler_params=_params(2),
        name="add_drivers",
    )(notes, _far(message))


def pick_tiles(group, slots, embedding, first_weight, second_weight, tile):
    groups, tiles = slots.shape
    rows, width = embedding.shape
    each = tiles // groups
    a, b = first_weight.shape[0], second_weight.shape[0]
    length = each * tile + a + b

    def body(group_ref, slots_ref, emb_ref, first_ref, second_ref, *rest):
        outs, (listed, sems) = rest[: groups - 1], rest[groups - 1 :]
        me = group_ref[0]
        copies = []
        for k in range(1, groups):
            out = outs[k - 1]
            other = (me + k) % groups
            copies.append(pltpu.make_async_copy(first_ref, out.at[pl.ds(each * tile, a), :], sems.at[k - 1, each]))
            copies.append(
                pltpu.make_async_copy(second_ref, out.at[pl.ds(each * tile + a, b), :], sems.at[k - 1, each + 1])
            )
            for j in range(each):
                listed[k - 1, j] = 0

            def look(t, found, k=k, other=other):
                tile_at = slots_ref[other, t]
                hit = (tile_at >= me * tiles) & (tile_at < (me + 1) * tiles)

                @pl.when(hit)
                def _():
                    listed[k - 1, jnp.minimum(found, each - 1)] = tile_at - me * tiles

                return found + hit.astype(I32)

            lax.fori_loop(0, tiles, look, jnp.zeros((), I32))
            for j in range(each):
                start = pl.multiple_of(listed[k - 1, j] * tile, tile)
                copies.append(
                    pltpu.make_async_copy(
                        emb_ref.at[pl.ds(start, tile), :], out.at[pl.ds(j * tile, tile), :], sems.at[k - 1, j]
                    )
                )
        for copy in copies:
            copy.start()
        for copy in copies:
            copy.wait()

    hbm = pl.BlockSpec(memory_space=pl.ANY)
    smem = pl.BlockSpec(memory_space=pltpu.SMEM)
    return pl.pallas_call(
        body,
        out_shape=[pltpu.HBM((length, width), BF16)] * (groups - 1),
        in_specs=[smem, smem, hbm, hbm, hbm],
        out_specs=[hbm] * (groups - 1),
        scratch_shapes=[
            pltpu.SMEM((groups - 1, each), I32),
            pltpu.SemaphoreType.DMA((groups - 1, each + 2)),
        ],
        compiler_params=_params(2),
        name="pick_tiles",
    )(group, slots, _near(embedding), first_weight, second_weight)


def ready(group, slot, embedding, arrived, first_weight, second_weight, tile):
    width = embedding.shape[1]
    tiles = slot.shape[0]
    groups = len(arrived) + 1
    each = tiles // groups
    a, b = first_weight.shape[0], second_weight.shape[0]

    def body(group_ref, slot_ref, emb_ref, own_a, own_b, *rest):
        parts = rest[: groups - 1]
        tiles_hbm, first_hbm, second_hbm, tiles_ref, first_ref, second_ref, tile_sems, sems, out_sems = rest[groups - 1 :]
        me = group_ref[0]
        firsts, seconds = [], []
        for k in range(groups):
            other = (me + groups - k) % groups
            from_a = own_a if k == 0 else parts[k - 1].at[pl.ds(each * tile, a), :]
            from_b = own_b if k == 0 else parts[k - 1].at[pl.ds(each * tile + a, b), :]
            to_a = first_ref.at[pl.ds(pl.multiple_of(other * a, a), a), :]
            to_b = second_ref.at[pl.ds(pl.multiple_of(other * b, b), b), :]
            firsts.append(pltpu.make_async_copy(from_a, to_a, sems.at[0, k]))
            seconds.append(pltpu.make_async_copy(from_b, to_b, sems.at[1, k]))

        def send(t, counts):
            tile_at = slot_ref[t]
            source = sum((tile_at >= tiles * g).astype(I32) for g in range(1, groups))
            spot = sum(jnp.where(source == g, counts[g], 0) for g in range(groups))
            away = (me + groups - source) % groups
            for k in range(groups):

                @pl.when(away == k)
                def _(k=k):
                    if k == 0:
                        at = pl.multiple_of((tile_at - source * tiles) * tile, tile)
                        here = emb_ref.at[pl.ds(at, tile), :]
                    else:
                        at = pl.multiple_of(jnp.minimum(spot, each - 1) * tile, tile)
                        here = parts[k - 1].at[pl.ds(at, tile), :]
                    pltpu.make_async_copy(here, tiles_ref.at[t], tile_sems.at[t]).start()

            return tuple(counts[g] + (source == g).astype(I32) for g in range(groups))

        lax.fori_loop(0, tiles, send, (jnp.zeros((), I32),) * groups)
        for copy in (*firsts, *seconds):
            copy.start()
        for t in range(tiles):
            pltpu.make_async_copy(emb_ref.at[pl.ds(0, tile), :], tiles_ref.at[t], tile_sems.at[t]).wait()
        leaving = [pltpu.make_async_copy(tiles_ref, tiles_hbm, out_sems.at[0])]
        leaving[-1].start()
        for n, (copies, here, there) in enumerate(
            ((firsts, first_ref, first_hbm), (seconds, second_ref, second_hbm)), start=1
        ):
            for copy in copies:
                copy.wait()
            leaving.append(pltpu.make_async_copy(here, there, out_sems.at[n]))
            leaving[-1].start()
        for copy in leaving:
            copy.wait()

    smem = pl.BlockSpec(memory_space=pltpu.SMEM)
    hbm = pl.BlockSpec(memory_space=pltpu.HBM)
    return pl.pallas_call(
        body,
        out_shape=[
            pltpu.HBM((tiles, tile, width), BF16),
            pltpu.HBM((groups * a, width), BF16),
            pltpu.HBM((groups * b, width), BF16),
        ],
        in_specs=[smem, smem, pl.BlockSpec(memory_space=pltpu.VMEM)] + [hbm] * (2 + len(arrived)),
        out_specs=[hbm] * 3,
        scratch_shapes=[
            pltpu.VMEM((tiles, tile, width), BF16),
            pltpu.VMEM((groups * a, width), BF16),
            pltpu.VMEM((groups * b, width), BF16),
            pltpu.SemaphoreType.DMA((tiles,)),
            pltpu.SemaphoreType.DMA((2, groups)),
            pltpu.SemaphoreType.DMA((3,)),
        ],
        compiler_params=_params(4),
        name="ready",
    )(group, slot, _near(embedding), *map(_far, (first_weight, second_weight, *arrived)))


def after_halo(
    halo_slot, halo, driver_at, local_tiles, adjacency, driver_weight, embedding, first, second, feats, feature_weight,
    first_bias, second_bias,
):
    rows, width = embedding.shape
    tiles, _, tile, _ = adjacency.shape
    doms, length, half = halo.shape
    cap = (length - 8) // 2
    hots = driver_weight.shape[1]
    many = tiles // 2
    block = many * tile
    per = tile // cap

    def body(local_hbm, adj_hbm, *rest):
        small_hbm, rest = rest[:7], rest[7:]
        halo_ref, at_ref, dw_ref, emb_ref, out_hbm, local_ref, adj_ref, *rest = rest
        small, (out, sems, in_sems, out_sems) = rest[:7], rest[7:]
        slot_ref, first_ref, feat_ref, fw_ref, first_bias_ref, second_ref, second_bias_ref = small
        blocks = tiles // many
        smalls = [pltpu.make_async_copy(x, y, sems.at[n]) for n, (x, y) in enumerate(zip(small_hbm, small))]
        smalls[0].start()
        arriving = []
        for n in range(blocks):
            these = pl.ds(n * many, many)
            arriving.append(
                (
                    pltpu.make_async_copy(local_hbm.at[these], local_ref.at[these], in_sems.at[0, n]),
                    pltpu.make_async_copy(adj_hbm.at[these], adj_ref.at[these], in_sems.at[1, n]),
                )
            )
            for copy in arriving[-1]:
                copy.start()
            if n == 0:
                for copy in smalls[1:]:
                    copy.start()
        column = lax.broadcasted_iota(I32, (hots, doms * 8), 1)
        ends = halo_ref[:, 2 * cap :, :].reshape(doms * 8, half)
        left = jnp.where(column == at_ref[...], 1.0, 0.0).astype(BF16)
        right = jnp.where(column == at_ref[...] + 4, 1.0, 0.0).astype(BF16)
        drivers = jnp.concatenate([_dot(left, ends).astype(BF16), _dot(right, ends).astype(BF16)], axis=1)
        smalls[0].wait()
        copies = []
        for n in range(blocks):
            if n == 0:
                for copy in arriving[0]:
                    copy.wait()
            aggregate = []
            for t in range(n * many, (n + 1) * many):
                which = pl.ds(pl.multiple_of(slot_ref[0, t] * per, per), per)
                halo_tile = jnp.concatenate(
                    [
                        halo_ref[which, :cap, :].reshape(tile, half),
                        halo_ref[which, cap : 2 * cap, :].reshape(tile, half),
                    ],
                    axis=1,
                )
                edges = jnp.concatenate([adj_ref[t, 0], adj_ref[t, 1], dw_ref[t * tile : (t + 1) * tile, :]], axis=1)
                sources = jnp.concatenate([local_ref[t], halo_tile, drivers], axis=0)
                aggregate.append(_dot(edges, sources).astype(BF16))
            if n == 0:
                for copy in (*smalls[1:], *arriving[1]):
                    copy.wait()
            here = slice(n * block, (n + 1) * block)
            own = emb_ref[here, :]
            inner = (
                _dot(jnp.concatenate([own, jnp.concatenate(aggregate, axis=0)], axis=1), first_ref[...])
                + lax.dot_general(
                    feat_ref[:, here], fw_ref[...], (((0,), (0,)), ((), ())), preferred_element_type=F32
                )
                + first_bias_ref[...]
            )
            activated = (0.5 * inner * (1.0 + lax.erf(inner * (0.5**0.5)))).astype(BF16)
            part = block // 2
            for h in range(2):
                there = slice(n * block + h * part, n * block + (h + 1) * part)
                out[there, :] = (
                    own[h * part : (h + 1) * part].astype(F32)
                    + second_bias_ref[...]
                    + _dot(activated[h * part : (h + 1) * part], second_ref[...])
                ).astype(BF16)
                copies.append(pltpu.make_async_copy(out.at[there, :], out_hbm.at[there, :], out_sems.at[2 * n + h]))
                copies[-1].start()
        for copy in copies:
            copy.wait()

    hbm = pl.BlockSpec(memory_space=pltpu.HBM)
    vmem = pl.BlockSpec(memory_space=pltpu.VMEM)
    smalls = (halo_slot.reshape(1, tiles), first, feats, feature_weight, first_bias, second, second_bias)
    return pl.pallas_call(
        body,
        out_shape=jax.ShapeDtypeStruct((rows, width), BF16),
        in_specs=[hbm] * 9 + [vmem] * 4,
        out_specs=hbm,
        scratch_shapes=[
            pltpu.VMEM(local_tiles.shape, BF16),
            pltpu.VMEM(adjacency.shape, BF16),
            pltpu.SMEM((1, tiles), I32),
            *[pltpu.VMEM(x.shape, x.dtype) for x in smalls[1:]],
            pltpu.VMEM((rows, width), BF16),
            pltpu.SemaphoreType.DMA((7,)),
            pltpu.SemaphoreType.DMA((2, tiles // many)),
            pltpu.SemaphoreType.DMA((2 * (tiles // many),)),
        ],
        compiler_params=_params(24),
        name="after_halo",
    )(
        *map(_far, (local_tiles, adjacency, *smalls)),
        *map(_near, (halo, driver_at, driver_weight, embedding)),
    )


def per_device(
    embedding,
    scenario_feats,
    adjacency,
    driver_weight,
    local_slot,
    halo_slot,
    send_rows,
    send_count,
    hot_ids,
    first_weight,
    feature_weight,
    first_bias,
    second_weight,
    second_bias,
):
    rows, width = embedding.shape
    tile = adjacency.shape[-1]
    tiles = rows // tile
    groups = lax.axis_size("scen")
    myself = lax.axis_index(("dom", "scen")).astype(I32).reshape(1)
    group = lax.axis_index("scen").astype(I32).reshape(1)

    page, embedding = note(myself, hot_ids, local_slot, embedding, groups)
    notes = lax.all_to_all(page, "scen", split_axis=0, concat_axis=0, tiled=True)
    message = pick_rows(send_rows, send_count, embedding)
    message = add_drivers(notes, message)
    halo = lax.all_to_all(message, "dom", split_axis=0, concat_axis=0, tiled=True)

    slots = notes[:, 1, :tiles].astype(I32)
    leaving = pick_tiles(group, slots, embedding, first_weight, second_weight, tile)
    arrived = [
        lax.ppermute(x, "scen", [(g, (g + k) % groups) for g in range(groups)])
        for k, x in enumerate(leaving, start=1)
    ]
    local_tiles, first, second = ready(group, local_slot, embedding, arrived, first_weight, second_weight, tile)
    owner = hot_ids // rows
    driver_at = (owner // groups * 8 + owner % groups).reshape(-1, 1)
    return after_halo(
        halo_slot,
        halo,
        driver_at,
        local_tiles,
        adjacency,
        driver_weight,
        embedding,
        first,
        second,
        scenario_feats,
        feature_weight,
        first_bias.reshape(1, width),
        second_bias.reshape(1, width),
    )


def solution(mesh):
    return jax.shard_map(
        per_device,
        mesh=mesh,
        in_specs=(
            P(("dom", "scen"), None),
            P(None, ("dom", "scen")),
            P(("dom", "scen"), None, None, None),
            P(("dom", "scen"), None),
            P(("dom", "scen")),
            P(("dom", "scen")),
            P(("dom", "scen"), None),
            P(("dom", "scen")),
            P(),
            P("scen", None),
            P(),
            P(),
            P("scen", None),
            P(),
        ),
        out_specs=P(("dom", "scen"), None),
        check_vma=False,
    )
```
